32 devices in a mesh: dp: 8 (over y, x, core), group: 4 (over z).
Axes of the slice: x: 2, y: 2, z: 4, core: 2. Of those that a mesh axis runs over, the one named last changes fastest.
Arguments:
- tokens: bfloat16 [8192, 640], P(('dp', 'group')), may hold values from -6 to 6
- cotangent: bfloat16 [8192, 640], P(('dp', 'group')), may hold values from -6 to 6
- positions: int32 [8192], P(('dp', 'group')), may hold values from 0 to 511, as said below
- attn_weights: float32 [12832, 128], P(('dp', 'group'))
- ffn_weights: float32 [30752, 128], P(('dp', 'group'))
- attn_m: float32 [12832, 128], P(('dp', 'group')), may hold values from -28 to 28
- attn_v: float32 [12832, 128], P(('dp', 'group')), may hold values from 9 to 82
- ffn_m: float32 [30752, 128], P(('dp', 'group')), may hold values from -28 to 28
- ffn_v: float32 [30752, 128], P(('dp', 'group')), may hold values from 9 to 82
Outputs:
- output: bfloat16 [8192, 640], P(('dp', 'group'))
- grad_tokens: float32 [8192, 640], P(('dp', 'group'))
- attn_grad: float32 [12832, 128], P(('dp', 'group'))
- ffn_grad: float32 [30752, 128], P(('dp', 'group'))
- attn_new: float32 [12832, 128], P(('dp', 'group'))
- ffn_new: float32 [30752, 128], P(('dp', 'group'))
- attn_m_new: float32 [12832, 128], P(('dp', 'group'))
- attn_v_new: float32 [12832, 128], P(('dp', 'group'))
- ffn_m_new: float32 [30752, 128], P(('dp', 'group'))
- ffn_v_new: float32 [30752, 128], P(('dp', 'group'))
The draws below stay inside these ranges and needn't reach their ends.
Inputs may be any that keep to these rules, and one draw needn't show every extreme that they name: Tokens come in sequences laid end to end; a token's position counts from its sequence's first token, so positions rise by one along a sequence. Each block of 1024 tokens along one group holds whole sequences, and every such block holds one sequence of exactly 512 tokens.
All inputs are finite; a program needn't handle non-finite values.
Results may differ from the reference program's by a relative error of at most 0.015.
The reference program's roundings to bfloat16 on the way count: a program that leaves them out, or rounds other values in their place, can miss the bound.
Values may be sent and summed in bfloat16 or wider, within the bound.
No kernel may reach another device: no remote copies, remote signals or barrier semaphores. Data moves between devices by JAX's collectives and lax.ppermute only.
A program may use at most 128 MiB of HBM per device.

```python
import math
import jax
import jax.numpy as jnp
from jax import lax

D = 640
H = 4
HD = 256
FF = 2048
WINDOW = 512
STEP = 3
TOK_DEV = 256
REACH = 2
GROUP_TOK = 1024
SEQ_MAX = 512
TOKENS = 8192
A_LEN = 12832
F_LEN = 30752


def base_noise(key, entries):
    return jax.random.normal(key, (entries,), jnp.float32)


def assemble(key, plan, full_rows):
    pieces = []
    filled = 0
    for number, (entries, spread) in enumerate(plan):
        pieces.append(base_noise(jax.random.fold_in(key, number), entries) * spread)
        filled = filled + entries
    pieces.append(base_noise(jax.random.fold_in(key, 99), full_rows * 128 - filled) * 0.02)
    return jnp.concatenate(pieces).reshape(full_rows, 128)


def draw_attn_weights(key, part):
    plan = [(D * H * HD, D ** (-0.5)), (D * HD, D ** (-0.5)), (D * HD, D ** (-0.5)), (H * HD * D, (H * HD) ** (-0.5)), (D, 0.1), (HD, 0.1), (HD, 0.1), (D, 0.1)]
    return assemble(key, plan, A_LEN)


def draw_ffn_weights(key, part):
    plan = [(D * FF, D ** (-0.5)), (D * FF, D ** (-0.5)), (FF * D, FF ** (-0.5)), (D, 0.1), (D, 0.1)]
    return assemble(key, plan, F_LEN)


def draw_positions(key, part):
    groups = TOKENS // GROUP_TOK
    start_key = jax.random.fold_in(key, 7001)
    offset_key = jax.random.fold_in(key, 7002)
    odds = max(2, SEQ_MAX // 8)
    offsets = jax.random.randint(offset_key, (groups, 1), 0, GROUP_TOK - SEQ_MAX + 1).astype(jnp.int32)
    index = jnp.arange(GROUP_TOK, dtype=jnp.int32)[None, :]
    coins = jax.random.randint(start_key, (groups, GROUP_TOK), 0, odds).astype(jnp.int32)
    inside_long = (index > offsets) & (index < offsets + SEQ_MAX)
    forced = (index == 0) | (index == offsets) | (index == offsets + SEQ_MAX)
    starts = ((coins == 0) | forced) & jnp.logical_not(inside_long)
    marks = jnp.where(starts, index, jnp.zeros_like(index))
    latest = lax.cummax(marks, axis=1)
    return (index - latest).reshape(TOKENS).astype(jnp.int32)


def block_levels(key, shape, cuts, smallest, top_value):
    loudness, own = 1.0, jax.random.fold_in(key, 6)
    for dim, parts in cuts:
        draws = jnp.exp(jax.random.uniform(jax.random.fold_in(own, dim), (parts,), jnp.float32, smallest / len(cuts), top_value / len(cuts)))
        loudness = loudness * jnp.repeat(draws, shape[dim] // parts).reshape([-1 if axis == dim else 1 for axis in range(len(shape))])
    return loudness


def bell_draw(stream_key, shape, scale, reach, cuts=(), kind=jnp.bfloat16):
    level = block_levels(stream_key, shape, cuts, -0.22, 0.18) if cuts else 1.0
    drawn = jax.random.normal(stream_key, shape, jnp.float32) * scale * level
    return jnp.minimum(jnp.maximum(drawn, -reach), reach).astype(kind)


def setup_inputs(seed: int = 0) -> dict:
    keys = jax.random.split(jax.random.key(seed), 10)
    return {
        "tokens": bell_draw(keys[0], (TOKENS, D), 1.0, 6.0, ((0, 32),)),
        "cotangent": bell_draw(keys[1], (TOKENS, D), 1.0, 6.0, ((0, 32),)),
        "positions": draw_positions(jax.random.fold_in(keys[9], 71), 0),
        "attn_weights": draw_attn_weights(jax.random.fold_in(keys[9], 71), 0),
        "ffn_weights": draw_ffn_weights(jax.random.fold_in(keys[9], 71), 0),
        "attn_m": bell_draw(keys[5], (A_LEN, 128), (0.05 * TOKENS ** 0.5), 28.0, ((0, 32),), jnp.float32),
        "attn_v": jnp.clip(jnp.exp(math.log(82.0) - 2.2094947 * jax.random.uniform(keys[6], (A_LEN, 128), jnp.float32) ** block_levels(keys[6], (A_LEN, 128), ((0, 32),), -0.2, 0.2)), 9.0, 82.0),
        "ffn_m": bell_draw(keys[7], (F_LEN, 128), (0.05 * TOKENS ** 0.5), 28.0, ((0, 32),), jnp.float32),
        "ffn_v": jnp.clip(jnp.exp(math.log(82.0) - 2.2094947 * jax.random.uniform(keys[8], (F_LEN, 128), jnp.float32) ** block_levels(keys[8], (F_LEN, 128), ((0, 32),), -0.2, 0.2)), 9.0, 82.0),
    }


NORM_EPS = 1e-06
THETA = 10000.0
BETA_ONE = 0.9
BETA_TWO = 0.95
LEARN_RATE = 0.02
WEIGHT_DECAY = 0.1
ADAM_EPS = 1e-08
GELU_COEF = 0.7978845608028654

def attn_shapes():
    return [(D, H * HD), (D, HD), (D, HD), (H * HD, D), (D,), (HD,), (HD,), (D,)]

def ffn_shapes():
    return [(D, FF), (D, FF), (FF, D), (D,), (D,)]

def split_flat(vector, dims_list):
    result = []
    offset = 0
    for dims_of in dims_list:
        length = 1
        for extent in dims_of:
            length = length * extent
        result.append(vector[offset:offset + length].reshape(dims_of))
        offset = offset + length
    return result

def pack_flat(arrays, full_rows):
    members = [member.reshape(-1).astype(jnp.float32) for member in arrays]
    filled = sum((member.shape[0] for member in members))
    members.append(jnp.zeros((full_rows * 128 - filled,), jnp.float32))
    return jnp.concatenate(members).reshape(full_rows, 128)

def norm_fwd(values, gain):
    recip = lax.rsqrt(lax.optimization_barrier(jnp.mean(values * values, axis=-1, keepdims=True)) + NORM_EPS)
    return (values * recip * (1.0 + gain), recip)

def norm_bwd(values, recip, gain, grad_out):
    scaled = grad_out * (1.0 + gain)
    grad_in = recip * scaled - values * recip * recip * recip * lax.optimization_barrier(jnp.mean(scaled * values, axis=-1, keepdims=True))
    grad_gain = lax.optimization_barrier(jnp.sum((grad_out * values * recip).reshape(-1, values.shape[-1]), axis=0))
    return (grad_in, grad_gain)

def rope_tables(positions):
    half_dim = HD // 2
    freqs = jnp.power(THETA, -2.0 * jnp.arange(half_dim, dtype=jnp.float32) / HD)
    angles = positions.astype(jnp.float32)[:, None] * freqs[None, :]
    return (jnp.cos(angles), jnp.sin(angles))

def rotate(values, cosine, sine_t):
    half_dim = values.shape[-1] // 2
    first, second = (values[..., :half_dim], values[..., half_dim:])
    return jnp.concatenate([first * cosine - second * sine_t, second * cosine + first * sine_t], axis=-1)

def rotate_back(grads_in, cosine, sine_t):
    half_dim = grads_in.shape[-1] // 2
    first, second = (grads_in[..., :half_dim], grads_in[..., half_dim:])
    return jnp.concatenate([first * cosine + second * sine_t, second * cosine - first * sine_t], axis=-1)

def gelu_pair(values):
    tangent = jnp.tanh(GELU_COEF * (values + 0.044715 * values ** 3))
    activated = 0.5 * values * (1.0 + tangent)
    slope_v = 0.5 * (1.0 + tangent) + 0.5 * values * (1.0 - tangent * tangent) * GELU_COEF * (1.0 + 3.0 * 0.044715 * values * values)
    return (activated, slope_v)

def cross_rows(left, right):
    return lax.dot_general(left, right, (((0,), (0,)), ((), ())), preferred_element_type=jnp.float32)

def times_trans(left, right):
    return lax.dot_general(left, right, (((1,), (1,)), ((), ())), preferred_element_type=jnp.float32)

def window_mask(query_count, key_count, positions):
    rows_i = jnp.arange(query_count, dtype=jnp.int32)[:, None] + (key_count - query_count)
    cols_j = jnp.arange(key_count, dtype=jnp.int32)[None, :]
    distance = rows_i - cols_j
    return (distance >= 0) & (distance <= jnp.minimum(positions, WINDOW - 1)[:, None])

def attend(query_b, window, positions):
    head_dim = query_b.shape[-1]
    key_b = window[:, :head_dim].astype(jnp.float32)
    value_b = window[:, head_dim:].astype(jnp.float32)
    visible = window_mask(query_b.shape[0], window.shape[0], positions)[None]
    scores = jnp.einsum('thd,kd->htk', query_b.astype(jnp.float32), key_b)
    log_total = jnp.log(lax.optimization_barrier(jnp.sum(jnp.where(visible, jnp.exp(scores), 0.0), axis=-1, keepdims=True)))
    attn_prob = jnp.where(visible, jnp.exp(scores - log_total), 0.0)
    prob_b = attn_prob.astype(jnp.bfloat16).astype(jnp.float32)
    attended = jnp.einsum('htk,kd->thd', prob_b, value_b)
    return (attended, log_total)

def attend_back(query_b, window, positions, log_total, grad_b):
    head_dim = query_b.shape[-1]
    key_b = window[:, :head_dim].astype(jnp.float32)
    value_b = window[:, head_dim:].astype(jnp.float32)
    query_f = query_b.astype(jnp.float32)
    grad_f = grad_b.astype(jnp.float32)
    visible = window_mask(query_b.shape[0], window.shape[0], positions)[None]
    scores = jnp.einsum('thd,kd->htk', query_f, key_b)
    attn_prob = jnp.where(visible, jnp.exp(scores - log_total), 0.0)
    prob_b = attn_prob.astype(jnp.bfloat16).astype(jnp.float32)
    grad_prob = jnp.einsum('thd,kd->htk', grad_f, value_b)
    row_dot = lax.optimization_barrier(jnp.sum(attn_prob * grad_prob, axis=-1, keepdims=True))
    grad_score = (attn_prob * (grad_prob - row_dot)).astype(jnp.bfloat16).astype(jnp.float32)
    grad_query = jnp.einsum('htk,kd->thd', grad_score, key_b)
    grad_key = jnp.einsum('htk,thd->kd', grad_score, query_f)
    grad_value = jnp.einsum('htk,thd->kd', prob_b, grad_f)
    return (grad_query, jnp.concatenate([grad_key, grad_value], axis=1))

def run_layer(tokens, cotangent, positions, attn_parts, fetch_ffn, send_ffn, attend_rows, attend_back_rows):
    w_q, w_k, w_v, w_o, g_in, g_q, g_k, g_mid = attn_parts
    gain_in = g_in.astype(jnp.float32)
    gain_q = g_q.astype(jnp.float32)
    gain_k = g_k.astype(jnp.float32)
    gain_mid = g_mid.astype(jnp.float32)
    row_count = tokens.shape[0]
    residual = tokens.astype(jnp.float32)
    normed, recip_in = norm_fwd(residual, gain_in)
    normed_b = normed.astype(jnp.bfloat16)
    queries = jnp.dot(normed_b, w_q, preferred_element_type=jnp.float32).reshape(row_count, H, HD)
    key_rows = jnp.dot(normed_b, w_k, preferred_element_type=jnp.float32)
    value_rows = jnp.dot(normed_b, w_v, preferred_element_type=jnp.float32)
    queries_n, recip_q = norm_fwd(queries, gain_q)
    keys_n, recip_k = norm_fwd(key_rows, gain_k)
    cosine, sine_t = rope_tables(positions)
    q_scale = HD ** (-0.5)
    query_b = (rotate(queries_n, cosine[:, None], sine_t[:, None]) * q_scale).astype(jnp.bfloat16)
    key_b = rotate(keys_n, cosine, sine_t).astype(jnp.bfloat16)
    kv_rows = jnp.concatenate([key_b, value_rows.astype(jnp.bfloat16)], axis=1)
    attended, kept_state = attend_rows(query_b, kv_rows, positions)
    attended_b = attended.reshape(row_count, H * HD).astype(jnp.bfloat16)
    branch = jnp.dot(attended_b, w_o, preferred_element_type=jnp.float32)
    branch_n, recip_mid = norm_fwd(branch, gain_mid)
    middle = residual + branch_n
    w_g, w_u, w_d, g_pre, g_post = fetch_ffn()
    gain_pre = g_pre.astype(jnp.float32)
    gain_post = g_post.astype(jnp.float32)
    pre_n, recip_pre = norm_fwd(middle, gain_pre)
    pre_b = pre_n.astype(jnp.bfloat16)
    gate_v = jnp.dot(pre_b, w_g, preferred_element_type=jnp.float32)
    upper = jnp.dot(pre_b, w_u, preferred_element_type=jnp.float32)
    activated, slope_v = gelu_pair(gate_v)
    hidden_b = (activated * upper).astype(jnp.bfloat16)
    ffn_out = jnp.dot(hidden_b, w_d, preferred_element_type=jnp.float32)
    ffn_n, recip_post = norm_fwd(ffn_out, gain_post)
    output = (middle + ffn_n).astype(jnp.bfloat16)
    grad_top = cotangent.astype(jnp.float32)
    grad_ffn, grad_post = norm_bwd(ffn_out, recip_post, gain_post, grad_top)
    grad_ffn_b = grad_ffn.astype(jnp.bfloat16)
    grad_wd = cross_rows(hidden_b, grad_ffn_b)
    grad_hidden = times_trans(grad_ffn_b, w_d)
    grad_gate_b = (grad_hidden * upper * slope_v).astype(jnp.bfloat16)
    grad_upper_b = (grad_hidden * activated).astype(jnp.bfloat16)
    grad_wg = cross_rows(pre_b, grad_gate_b)
    grad_wu = cross_rows(pre_b, grad_upper_b)
    grad_pre_in = times_trans(grad_gate_b, w_g) + times_trans(grad_upper_b, w_u)
    grad_mid_add, grad_pre = norm_bwd(middle, recip_pre, gain_pre, grad_pre_in)
    grad_middle = grad_top + grad_mid_add
    ffn_result = send_ffn([grad_wg, grad_wu, grad_wd, grad_pre, grad_post])
    grad_branch, grad_gmid = norm_bwd(branch, recip_mid, gain_mid, grad_middle)
    grad_branch_b = grad_branch.astype(jnp.bfloat16)
    grad_wo = cross_rows(attended_b, grad_branch_b)
    grad_att_b = times_trans(grad_branch_b, w_o).reshape(row_count, H, HD).astype(jnp.bfloat16)
    grad_query, grad_kv = attend_back_rows(kept_state, grad_att_b)
    grad_qn = rotate_back(grad_query * q_scale, cosine[:, None], sine_t[:, None])
    grad_q, grad_gq = norm_bwd(queries, recip_q, gain_q, grad_qn)
    grad_kn = rotate_back(grad_kv[:, :HD], cosine, sine_t)
    grad_k, grad_gk = norm_bwd(key_rows, recip_k, gain_k, grad_kn)
    grad_q_b = grad_q.reshape(row_count, H * HD).astype(jnp.bfloat16)
    grad_k_b = grad_k.astype(jnp.bfloat16)
    grad_v_b = grad_kv[:, HD:].astype(jnp.bfloat16)
    grad_wq = cross_rows(normed_b, grad_q_b)
    grad_wk = cross_rows(normed_b, grad_k_b)
    grad_wv = cross_rows(normed_b, grad_v_b)
    grad_normed = times_trans(grad_q_b, w_q) + times_trans(grad_k_b, w_k) + times_trans(grad_v_b, w_v)
    grad_in_add, grad_gin = norm_bwd(residual, recip_in, gain_in, grad_normed)
    grad_tokens = grad_middle + grad_in_add
    attn_grads = [grad_wq, grad_wk, grad_wv, grad_wo, grad_gin, grad_gq, grad_gk, grad_gmid]
    return (output, grad_tokens, attn_grads, ffn_result)

def adam_step(param, grad_in, moment_one, moment_two):
    new_one = BETA_ONE * moment_one + (1.0 - BETA_ONE) * grad_in
    new_two = BETA_TWO * moment_two + (1.0 - BETA_TWO) * grad_in * grad_in
    corr_one = new_one / (1.0 - BETA_ONE ** STEP)
    corr_two = new_two / (1.0 - BETA_TWO ** STEP)
    new_param = param - LEARN_RATE * (corr_one / (jnp.sqrt(corr_two) + ADAM_EPS) + WEIGHT_DECAY * param)
    return (new_param, new_one, new_two)

def group_attend(query_b, kv_rows, positions):
    blocks = query_b.shape[0] // TOK_DEV
    span = (REACH + 1) * TOK_DEV
    padded = jnp.concatenate([jnp.zeros((REACH * TOK_DEV, kv_rows.shape[1]), jnp.bfloat16), kv_rows], axis=0)
    index = (jnp.arange(blocks, dtype=jnp.int32) * TOK_DEV)[:, None] + jnp.arange(span, dtype=jnp.int32)[None, :]
    windows = padded[index]
    block_q = query_b.reshape(blocks, TOK_DEV, H, HD)
    block_pos = positions.reshape(blocks, TOK_DEV)
    attended, log_total = jax.vmap(attend)(block_q, windows, block_pos)
    return (attended.reshape(query_b.shape), (block_q, windows, block_pos, log_total, index))

def group_attend_back(kept_state, grad_b):
    block_q, windows, block_pos, log_total, index = kept_state
    grad_blocks = grad_b.reshape(block_q.shape)
    grad_query, grad_window = jax.vmap(attend_back)(block_q, windows, block_pos, log_total, grad_blocks)
    total_rows = index.shape[0] * TOK_DEV + REACH * TOK_DEV
    summed = jnp.zeros((total_rows, windows.shape[-1]), jnp.float32).at[index].add(grad_window)
    return (grad_query.reshape(grad_b.shape), summed[REACH * TOK_DEV:])

def reference(tokens, cotangent, positions, attn_weights, ffn_weights, attn_m, attn_v, ffn_m, ffn_v):
    attn_parts = split_flat(attn_weights.astype(jnp.bfloat16).reshape(-1), attn_shapes())
    ffn_parts = split_flat(ffn_weights.astype(jnp.bfloat16).reshape(-1), ffn_shapes())
    groups = TOKENS // GROUP_TOK

    def one_group(carry, member):
        tok_rows, cot_rows, pos_rows = member
        output, grad_tokens, attn_grads, ffn_grads = run_layer(tok_rows, cot_rows, pos_rows, attn_parts, lambda: ffn_parts, lambda grad_list: grad_list, group_attend, group_attend_back)
        return ((carry[0] + pack_flat(attn_grads, A_LEN), carry[1] + pack_flat(ffn_grads, F_LEN)), (output, grad_tokens))
    initial = (jnp.zeros((A_LEN, 128), jnp.float32), jnp.zeros((F_LEN, 128), jnp.float32))
    stacked = (tokens.reshape(groups, GROUP_TOK, D), cotangent.reshape(groups, GROUP_TOK, D), positions.reshape(groups, GROUP_TOK))
    (attn_grad, ffn_grad), (outputs, grad_rows) = lax.scan(one_group, initial, stacked)
    attn_new, attn_m_new, attn_v_new = adam_step(attn_weights, attn_grad, attn_m, attn_v)
    ffn_new, ffn_m_new, ffn_v_new = adam_step(ffn_weights, ffn_grad, ffn_m, ffn_v)
    return (outputs.reshape(TOKENS, D), grad_rows.reshape(TOKENS, D), attn_grad, ffn_grad, attn_new, ffn_new, attn_m_new, attn_v_new, ffn_m_new, ffn_v_new)
```

```python
import functools
import math

import jax
import jax.numpy as jnp
from jax import lax
from jax.experimental import pallas as pl
from jax.experimental.pallas import tpu as pltpu
from jax.sharding import PartitionSpec as P

D = 640
H = 4
HD = 256
FF = 2048
WINDOW = 512
STEP = 3


NORM_EPS = 1e-06
THETA = 10000.0
BETA_ONE = 0.9
BETA_TWO = 0.95
LEARN_RATE = 0.02
WEIGHT_DECAY = 0.1
ADAM_EPS = 1e-08
GELU_COEF = 0.7978845608028654


def passed_along(shard, axis, by):
    count = lax.axis_size(axis)
    pairs = [(i, i + by) for i in range(count) if 0 <= i + by < count]
    return lax.ppermute(shard, axis, pairs)


def attn_shapes():
    return [(D, H * HD), (D, HD), (D, HD), (H * HD, D), (D,), (HD,), (HD,), (D,)]


def ffn_shapes():
    return [(D, FF), (D, FF), (FF, D), (D,), (D,)]


def split_flat(vector, dims_list):
    result = []
    offset = 0
    for dims_of in dims_list:
        length = 1
        for extent in dims_of:
            length = length * extent
        result.append(vector[offset : offset + length].reshape(dims_of))
        offset = offset + length
    return result


def norm_fwd(values, gain):
    recip = lax.rsqrt(jnp.mean(values * values, axis=-1, keepdims=True) + NORM_EPS)
    return (values * recip * (1.0 + gain), recip)


def norm_bwd(values, recip, gain, grad_out):
    scaled = grad_out * (1.0 + gain)
    grad_in = recip * scaled - values * recip * recip * recip * jnp.mean(
        scaled * values, axis=-1, keepdims=True
    )
    grad_gain = jnp.sum((grad_out * values * recip).reshape(-1, values.shape[-1]), axis=0)
    return (grad_in, grad_gain)


def rope_tables(positions):
    half_dim = HD // 2
    freqs = jnp.power(THETA, -2.0 * jnp.arange(half_dim, dtype=jnp.float32) / HD)
    angles = positions.astype(jnp.float32)[:, None] * freqs[None, :]
    return (jnp.cos(angles), jnp.sin(angles))


def rotate(values, cosine, sine_t):
    half_dim = values.shape[-1] // 2
    first, second = (values[..., :half_dim], values[..., half_dim:])
    return jnp.concatenate(
        [first * cosine - second * sine_t, second * cosine + first * sine_t], axis=-1
    )


def rotate_back(grads_in, cosine, sine_t):
    half_dim = grads_in.shape[-1] // 2
    first, second = (grads_in[..., :half_dim], grads_in[..., half_dim:])
    return jnp.concatenate(
        [first * cosine + second * sine_t, second * cosine - first * sine_t], axis=-1
    )


def gelu_pair(values):
    tangent = jnp.tanh(GELU_COEF * (values + 0.044715 * values**3))
    activated = 0.5 * values * (1.0 + tangent)
    slope_v = 0.5 * (1.0 + tangent) + 0.5 * values * (1.0 - tangent * tangent) * GELU_COEF * (
        1.0 + 3.0 * 0.044715 * values * values
    )
    return (activated, slope_v)


def times_trans(left, right):
    return lax.dot_general(
        left, right, (((1,), (1,)), ((), ())), preferred_element_type=jnp.float32
    )


def window_mask(query_count, key_count, positions):
    rows_i = jnp.arange(query_count, dtype=jnp.int32)[:, None] + (key_count - query_count)
    cols_j = jnp.arange(key_count, dtype=jnp.int32)[None, :]
    distance = rows_i - cols_j
    return (distance >= 0) & (distance <= jnp.minimum(positions, WINDOW - 1)[:, None])


def attend(query_b, window, positions):
    head_dim = query_b.shape[-1]
    key_b = window[:, :head_dim]
    value_b = window[:, head_dim:]
    visible = window_mask(query_b.shape[0], window.shape[0], positions)[None]
    scores = jnp.einsum("thd,kd->htk", query_b, key_b, preferred_element_type=jnp.float32)
    log_total = jnp.log(jnp.sum(jnp.where(visible, jnp.exp(scores), 0.0), axis=-1, keepdims=True))
    attn_prob = jnp.where(visible, jnp.exp(scores - log_total), 0.0)
    prob_b = attn_prob.astype(jnp.bfloat16)
    attended = jnp.einsum("htk,kd->thd", prob_b, value_b, preferred_element_type=jnp.float32)
    return (attended, log_total)


def attend_back(query_b, window, positions, log_total, grad_b):
    head_dim = query_b.shape[-1]
    key_b = window[:, :head_dim]
    value_b = window[:, head_dim:]
    visible = window_mask(query_b.shape[0], window.shape[0], positions)[None]
    scores = jnp.einsum("thd,kd->htk", query_b, key_b, preferred_element_type=jnp.float32)
    attn_prob = jnp.where(visible, jnp.exp(scores - log_total), 0.0)
    prob_b = attn_prob.astype(jnp.bfloat16)
    grad_prob = jnp.einsum("thd,kd->htk", grad_b, value_b, preferred_element_type=jnp.float32)
    row_dot = jnp.sum(attn_prob * grad_prob, axis=-1, keepdims=True)
    grad_score = (attn_prob * (grad_prob - row_dot)).astype(jnp.bfloat16)
    grad_query = jnp.einsum("htk,kd->thd", grad_score, key_b, preferred_element_type=jnp.float32)
    grad_key = jnp.einsum("htk,thd->kd", grad_score, query_b, preferred_element_type=jnp.float32)
    grad_value = jnp.einsum("htk,thd->kd", prob_b, grad_b, preferred_element_type=jnp.float32)
    return (grad_query, jnp.concatenate([grad_key, grad_value], axis=1))


def run_layer(
    tokens, cotangent, positions, attn_parts, fetch_ffn, send_ffn, send_attn, attend_rows, attend_back_rows
):
    w_q, w_k, w_v, w_o, g_in, g_q, g_k, g_mid = attn_parts
    gain_in = g_in.astype(jnp.float32)
    gain_q = g_q.astype(jnp.float32)
    gain_k = g_k.astype(jnp.float32)
    gain_mid = g_mid.astype(jnp.float32)
    row_count = tokens.shape[0]
    residual = tokens.astype(jnp.float32)
    normed, recip_in = norm_fwd(residual, gain_in)
    normed_b = normed.astype(jnp.bfloat16)
    queries = jnp.dot(normed_b, w_q, preferred_element_type=jnp.float32).reshape(row_count, H, HD)
    key_rows = jnp.dot(normed_b, w_k, preferred_element_type=jnp.float32)
    value_rows = jnp.dot(normed_b, w_v, preferred_element_type=jnp.float32)
    queries_n, recip_q = norm_fwd(queries, gain_q)
    keys_n, recip_k = norm_fwd(key_rows, gain_k)
    cosine, sine_t = rope_tables(positions)
    q_scale = HD ** (-0.5)
    query_b = (rotate(queries_n, cosine[:, None], sine_t[:, None]) * q_scale).astype(jnp.bfloat16)
    key_b = rotate(keys_n, cosine, sine_t).astype(jnp.bfloat16)
    kv_rows = jnp.concatenate([key_b, value_rows.astype(jnp.bfloat16)], axis=1)
    attended, kept_state = attend_rows(query_b, kv_rows, positions)
    attended_b = attended.reshape(row_count, H * HD).astype(jnp.bfloat16)
    branch = jnp.dot(attended_b, w_o, preferred_element_type=jnp.float32)
    branch_n, recip_mid = norm_fwd(branch, gain_mid)
    middle = residual + branch_n
    w_g, w_u, w_d, g_pre, g_post = fetch_ffn()
    gain_pre = g_pre.astype(jnp.float32)
    gain_post = g_post.astype(jnp.float32)
    pre_n, recip_pre = norm_fwd(middle, gain_pre)
    pre_b = pre_n.astype(jnp.bfloat16)
    gate_v = jnp.dot(pre_b, w_g, preferred_element_type=jnp.float32)
    upper = jnp.dot(pre_b, w_u, preferred_element_type=jnp.float32)
    activated, slope_v = gelu_pair(gate_v)
    hidden_b = (activated * upper).astype(jnp.bfloat16)
    ffn_out = jnp.dot(hidden_b, w_d, preferred_element_type=jnp.float32)
    ffn_n, recip_post = norm_fwd(ffn_out, gain_post)
    output = (middle + ffn_n).astype(jnp.bfloat16)
    grad_top = cotangent.astype(jnp.float32)
    grad_ffn, grad_post = norm_bwd(ffn_out, recip_post, gain_post, grad_top)
    grad_ffn_b = grad_ffn.astype(jnp.bfloat16)
    grad_hidden = times_trans(grad_ffn_b, w_d)
    grad_gate_b = (grad_hidden * upper * slope_v).astype(jnp.bfloat16)
    grad_upper_b = (grad_hidden * activated).astype(jnp.bfloat16)
    grad_pre_in = times_trans(grad_gate_b, w_g) + times_trans(grad_upper_b, w_u)
    grad_mid_add, grad_pre = norm_bwd(middle, recip_pre, gain_pre, grad_pre_in)
    grad_middle = grad_top + grad_mid_add
    ffn_result = send_ffn(
        [pre_b, pre_b, hidden_b],
        [grad_gate_b, grad_upper_b, grad_ffn_b],
        jnp.concatenate([grad_pre, grad_post]).reshape(-1, 128),
    )
    grad_branch, grad_gmid = norm_bwd(branch, recip_mid, gain_mid, grad_middle)
    grad_branch_b = grad_branch.astype(jnp.bfloat16)
    grad_att_b = times_trans(grad_branch_b, w_o).reshape(row_count, H, HD).astype(jnp.bfloat16)
    grad_query, grad_kv = attend_back_rows(kept_state, grad_att_b)
    grad_qn = rotate_back(grad_query * q_scale, cosine[:, None], sine_t[:, None])
    grad_q, grad_gq = norm_bwd(queries, recip_q, gain_q, grad_qn)
    grad_kn = rotate_back(grad_kv[:, :HD], cosine, sine_t)
    grad_k, grad_gk = norm_bwd(key_rows, recip_k, gain_k, grad_kn)
    grad_q_b = grad_q.reshape(row_count, H * HD).astype(jnp.bfloat16)
    grad_k_b = grad_k.astype(jnp.bfloat16)
    grad_v_b = grad_kv[:, HD:].astype(jnp.bfloat16)
    grad_normed = (
        times_trans(grad_q_b, w_q) + times_trans(grad_k_b, w_k) + times_trans(grad_v_b, w_v)
    )
    grad_in_add, grad_gin = norm_bwd(residual, recip_in, gain_in, grad_normed)
    grad_tokens = grad_middle + grad_in_add
    attn_result = send_attn(
        [normed_b, normed_b, normed_b, attended_b],
        [grad_q_b, grad_k_b, grad_v_b, grad_branch_b],
        jnp.concatenate([grad_gin, grad_gq, grad_gk, grad_gmid]).reshape(-1, 128),
    )
    return (output, grad_tokens, attn_result, ffn_result)


def adam_step(param, grad_in, moment_one, moment_two):
    new_one = BETA_ONE * moment_one + (1.0 - BETA_ONE) * grad_in
    new_two = BETA_TWO * moment_two + (1.0 - BETA_TWO) * grad_in * grad_in
    corr_one = new_one / (1.0 - BETA_ONE**STEP)
    corr_two = new_two / (1.0 - BETA_TWO**STEP)
    new_param = param - LEARN_RATE * (
        corr_one / (jnp.sqrt(corr_two) + ADAM_EPS) + WEIGHT_DECAY * param
    )
    return (new_param, new_one, new_two)


def device_attend(query_b, kv_rows, positions):
    tok_rows = kv_rows.shape[0]
    reach = (WINDOW - 1) // tok_rows + 1
    pieces = []
    for shift_by in range(reach, 0, -1):
        pieces.append(passed_along(kv_rows, "group", shift_by))
    window = jnp.concatenate(pieces + [kv_rows], axis=0)
    attended, log_total = attend(query_b, window, positions)
    return (attended, (query_b, window, positions, log_total))


def device_attend_back(kept_state, grad_b):
    query_b, window, positions, log_total = kept_state
    grad_query, grad_window = attend_back(query_b, window, positions, log_total, grad_b)
    tok_rows = query_b.shape[0]
    reach = window.shape[0] // tok_rows - 1
    totals = grad_window[reach * tok_rows :]
    for shift_by in range(reach, 0, -1):
        slot_idx = reach - shift_by
        piece = grad_window[slot_idx * tok_rows : (slot_idx + 1) * tok_rows]
        totals = totals + passed_along(piece.astype(jnp.bfloat16), "group", -shift_by).astype(
            piece.dtype
        )
    return (grad_query, totals)


BF = jnp.bfloat16
F32 = jnp.float32
VMEM_LIMIT = 60 * 1024 * 1024


def rows_up(count, unit=16):
    return -(-count // unit) * unit


def pack_body(jobs, own, padded, sizes, core_ref, *refs):
    count = len(jobs)
    lefts, rights, gains = refs[:count], refs[count : 2 * count], refs[2 * count]
    send_ref, keep_ref, flat = refs[2 * count + 1 :]
    offset = 0
    tile = 128
    for (m, n), left, right in zip(jobs, lefts, rights):
        per_row = n // 128

        def step(i, carry, left=left, right=right, per_row=per_row, offset=offset):
            start = pl.multiple_of(i * tile, tile)
            block = lax.dot_general(
                left[:, pl.ds(start, tile)],
                right[...],
                (((0,), (0,)), ((), ())),
                preferred_element_type=F32,
            )
            base = offset + i * (tile * per_row)
            for j in range(per_row):
                flat[pl.ds(base + j, tile, stride=per_row), :] = block[:, 128 * j : 128 * j + 128]
            return carry

        lax.fori_loop(0, m // tile, step, 0)
        offset = offset + m * per_row
    tail = flat.shape[0] - offset
    flat[pl.ds(offset, tail), :] = jnp.zeros((tail, 128), F32)
    flat[pl.ds(offset, gains.shape[0]), :] = gains[...]
    slow, fast, cores, depth = sizes
    half = slow * fast * depth
    core = core_ref[0]

    def cut(i, carry):
        lead, z = i // depth, i % depth
        mine = ((lead * 2 + core) * depth + z) * own
        other = ((lead * 2 + 1 - core) * depth + z) * own
        keep_ref[i] = flat[pl.ds(mine, padded), :].astype(BF)
        send_ref[i] = flat[pl.ds(other, padded), :].astype(BF)
        return carry

    lax.fori_loop(0, half, cut, 0)


def pack_grads(jobs, lefts, rights, gains, own, sizes, core):
    padded = rows_up(own)
    devices = math.prod(sizes)
    half = devices // 2
    whole = rows_up(devices * own + 16, 8)
    out = jax.ShapeDtypeStruct((half, padded, 128), BF)
    vmem = pl.BlockSpec(memory_space=pltpu.VMEM)
    flops = sum(2 * m * n * lefts[0].shape[0] for m, n in jobs)
    return pl.pallas_call(
        functools.partial(pack_body, jobs, own, padded, sizes),
        out_shape=(out, out),
        in_specs=[pl.BlockSpec(memory_space=pltpu.SMEM)] + [vmem] * (2 * len(jobs) + 1),
        out_specs=(vmem, vmem),
        scratch_shapes=[pltpu.VMEM((whole, 128), F32)],
        compiler_params=pltpu.CompilerParams(vmem_limit_bytes=VMEM_LIMIT),
        cost_estimate=pl.CostEstimate(
            flops=flops, bytes_accessed=devices * padded * 256, transcendentals=0
        ),
    )(core, *lefts, *rights, gains)


def grid_of():
    pairs = lax.axis_size("dp") // 2
    slow = math.isqrt(pairs)
    fast = pairs // slow
    depth = lax.axis_size("group")
    place = lax.axis_index("dp")
    where = (place // (2 * fast), (place // 2) % fast, place % 2, lax.axis_index("group"))
    return ((slow, fast, 2, depth), where)


def step_along(value, axis, by, sizes, senders=None):
    extent = sizes[axis]
    pairs = []
    if axis == 3:
        for i in range(extent):
            if 0 <= i + by < extent and (senders is None or i in senders):
                pairs.append((i, i + by))
        return lax.ppermute(value, "group", pairs)
    stride = (2 * sizes[1], 2, 1)[axis]
    for i in range(sizes[0] * sizes[1] * 2):
        at = (i // stride) % extent
        if 0 <= at + by < extent and (senders is None or at in senders):
            pairs.append((i, i + by * stride))
    return lax.ppermute(value, "dp", pairs)


def swap_along(value, axis, sizes):
    stride = (2 * sizes[1], 2, 1)[axis]
    count = sizes[0] * sizes[1] * 2
    pairs = [(i, i + stride * (1 - 2 * ((i // stride) % 2))) for i in range(count)]
    return lax.ppermute(value, "dp", pairs)


def pick(blocks, index):
    return lax.dynamic_index_in_dim(blocks, index, axis=0, keepdims=False)


def scatter_axis(blocks, axis, sizes, where):
    extent, at = (sizes[axis], where[axis])
    if extent == 1:
        return blocks[0].astype(jnp.float32)
    if extent == 2 and axis < 3:
        arrived = swap_along(pick(blocks, 1 - at), axis, sizes)
        return pick(blocks, at).astype(jnp.float32) + arrived.astype(jnp.float32)
    total = pick(blocks, at).astype(jnp.float32)
    for by in (1, -1):
        arrived = None
        for step in range(1, extent):
            dest = jnp.clip(at + by * (extent - step), 0, extent - 1)
            load = pick(blocks, dest)
            if arrived is not None:
                load = (load.astype(jnp.float32) + arrived.astype(jnp.float32)).astype(jnp.bfloat16)
            senders = range(step) if by == 1 else range(extent - step, extent)
            arrived = step_along(load, axis, by, sizes, senders)
        total = total + arrived.astype(jnp.float32)
    return total


def after_core(pair, sizes):
    send, keep = pair
    arrived = swap_along(send, 2, sizes)
    total = (keep.astype(F32) + arrived.astype(F32)).astype(BF)
    return total.reshape(sizes[0], sizes[1], sizes[3], *send.shape[1:])


def scatter_sum(attn_pair, ffn_pair, sizes, where):
    attn_held = after_core(attn_pair, sizes)
    ffn_held = after_core(ffn_pair, sizes)
    attn_rows, ffn_rows = attn_held.shape[3], ffn_held.shape[3]
    cut = (attn_rows + ffn_rows) // 32 * 16
    first = ffn_held[:, :, :, :cut]
    second = jnp.concatenate([ffn_held[:, :, :, cut:], attn_held], axis=3)
    second = second.transpose(1, 0, 2, 3, 4)
    first = scatter_axis(first, 0, sizes, where).astype(BF)
    second = scatter_axis(second, 1, sizes, where).astype(BF)
    first = scatter_axis(first, 1, sizes, where).astype(BF)
    second = scatter_axis(second, 0, sizes, where).astype(BF)
    summed = scatter_axis(jnp.concatenate([first, second], axis=1), 3, sizes, where)
    return (summed[ffn_rows:], summed[:ffn_rows])


def shards(tokens, cotangent, positions, attn_weights, ffn_weights, attn_m, attn_v, ffn_m, ffn_v):
    attn_full, ffn_full = (
        lax.all_gather(attn_weights.astype(jnp.bfloat16), ("dp", "group"), axis=0, tiled=True),
        lax.all_gather(ffn_weights.astype(jnp.bfloat16), ("dp", "group"), axis=0, tiled=True),
    )
    attn_parts = split_flat(attn_full.reshape(-1), attn_shapes())

    def fetch_ffn():
        return split_flat(ffn_full.reshape(-1), ffn_shapes())

    sizes, where = grid_of()
    core = where[2].astype(jnp.int32).reshape(1)
    attn_own, ffn_own = (attn_weights.shape[0], ffn_weights.shape[0])

    def send_ffn(lefts, rights, gains):
        return pack_grads(ffn_shapes()[:3], lefts, rights, gains, ffn_own, sizes, core)

    def send_attn(lefts, rights, gains):
        return pack_grads(attn_shapes()[:4], lefts, rights, gains, attn_own, sizes, core)

    output, grad_tokens, attn_result, ffn_result = run_layer(
        tokens,
        cotangent,
        positions,
        attn_parts,
        fetch_ffn,
        send_ffn,
        send_attn,
        device_attend,
        device_attend_back,
    )
    attn_grad, ffn_grad = scatter_sum(attn_result, ffn_result, sizes, where)
    attn_grad, ffn_grad = (attn_grad[:attn_own], ffn_grad[:ffn_own])
    attn_new, attn_m_new, attn_v_new = adam_step(attn_weights, attn_grad, attn_m, attn_v)
    ffn_new, ffn_m_new, ffn_v_new = adam_step(ffn_weights, ffn_grad, ffn_m, ffn_v)
    return (
        output,
        grad_tokens,
        attn_grad,
        ffn_grad,
        attn_new,
        ffn_new,
        attn_m_new,
        attn_v_new,
        ffn_m_new,
        ffn_v_new,
    )


def solution(mesh):
    placed = (
        P(("dp", "group"), None),
        P(("dp", "group"), None),
        P(("dp", "group")),
        P(("dp", "group"), None),
        P(("dp", "group"), None),
        P(("dp", "group"), None),
        P(("dp", "group"), None),
        P(("dp", "group"), None),
        P(("dp", "group"), None),
    )
    return jax.shard_map(
        shards,
        mesh=mesh,
        in_specs=placed,
        out_specs=(
            P(("dp", "group"), None),
            P(("dp", "group"), None),
            P(("dp", "group"), None),
            P(("dp", "group"), None),
            P(("dp", "group"), None),
            P(("dp", "group"), None),
            P(("dp", "group"), None),
            P(("dp", "group"), None),
            P(("dp", "group"), None),
            P(("dp", "group"), None),
        ),
        check_vma=False,
    )
```

```python
import functools
import math

import jax
import jax.numpy as jnp
from jax import lax
from jax.experimental import pallas as pl
from jax.experimental.pallas import tpu as pltpu
from jax.sharding import PartitionSpec as P

D = 640
H = 4
HD = 256
FF = 2048
WINDOW = 512
STEP = 3


NORM_EPS = 1e-06
THETA = 10000.0
BETA_ONE = 0.9
BETA_TWO = 0.95
LEARN_RATE = 0.02
WEIGHT_DECAY = 0.1
ADAM_EPS = 1e-08
GELU_COEF = 0.7978845608028654


def passed_along(shard, axis, by):
    count = lax.axis_size(axis)
    pairs = [(i, i + by) for i in range(count) if 0 <= i + by < count]
    return lax.ppermute(shard, axis, pairs)


def attn_shapes():
    return [(D, H * HD), (D, HD), (D, HD), (H * HD, D), (D,), (HD,), (HD,), (D,)]


def ffn_shapes():
    return [(D, FF), (D, FF), (FF, D), (D,), (D,)]


def norm_fwd(values, gain):
    recip = lax.rsqrt(jnp.mean(values * values, axis=-1, keepdims=True) + NORM_EPS)
    return (values * recip * (1.0 + gain), recip)


def norm_bwd(values, recip, gain, grad_out):
    scaled = grad_out * (1.0 + gain)
    grad_in = recip * scaled - values * recip * recip * recip * jnp.mean(
        scaled * values, axis=-1, keepdims=True
    )
    grad_gain = jnp.sum((grad_out * values * recip).reshape(-1, values.shape[-1]), axis=0)
    return (grad_in, grad_gain)


def rope_tables(positions):
    half_dim = HD // 2
    freqs = jnp.power(THETA, -2.0 * jnp.arange(half_dim, dtype=jnp.float32) / HD)
    angles = positions.astype(jnp.float32)[:, None] * freqs[None, :]
    return (jnp.cos(angles), jnp.sin(angles))


def rotate(values, cosine, sine_t):
    half_dim = values.shape[-1] // 2
    first, second = (values[..., :half_dim], values[..., half_dim:])
    return jnp.concatenate(
        [first * cosine - second * sine_t, second * cosine + first * sine_t], axis=-1
    )


def rotate_back(grads_in, cosine, sine_t):
    half_dim = grads_in.shape[-1] // 2
    first, second = (grads_in[..., :half_dim], grads_in[..., half_dim:])
    return jnp.concatenate(
        [first * cosine + second * sine_t, second * cosine - first * sine_t], axis=-1
    )


def gelu_pair(values):
    tangent = jnp.tanh(GELU_COEF * (values + 0.044715 * values**3))
    activated = 0.5 * values * (1.0 + tangent)
    slope_v = 0.5 * (1.0 + tangent) + 0.5 * values * (1.0 - tangent * tangent) * GELU_COEF * (
        1.0 + 3.0 * 0.044715 * values * values
    )
    return (activated, slope_v)


def times_trans(left, right):
    return lax.dot_general(
        left, right, (((1,), (1,)), ((), ())), preferred_element_type=jnp.float32
    )


def window_mask(query_count, key_count, positions):
    rows_i = jnp.arange(query_count, dtype=jnp.int32)[:, None] + (key_count - query_count)
    cols_j = jnp.arange(key_count, dtype=jnp.int32)[None, :]
    distance = rows_i - cols_j
    return (distance >= 0) & (distance <= jnp.minimum(positions, WINDOW - 1)[:, None])


def attend(query_b, window, positions):
    head_dim = query_b.shape[-1]
    key_b = window[:, :head_dim]
    value_b = window[:, head_dim:]
    visible = window_mask(query_b.shape[0], window.shape[0], positions)[None]
    scores = jnp.einsum("thd,kd->htk", query_b, key_b, preferred_element_type=jnp.float32)
    log_total = jnp.log(jnp.sum(jnp.where(visible, jnp.exp(scores), 0.0), axis=-1, keepdims=True))
    attn_prob = jnp.where(visible, jnp.exp(scores - log_total), 0.0)
    prob_b = attn_prob.astype(jnp.bfloat16)
    attended = jnp.einsum("htk,kd->thd", prob_b, value_b, preferred_element_type=jnp.float32)
    return (attended, log_total)


def attend_back(query_b, window, positions, log_total, grad_b):
    head_dim = query_b.shape[-1]
    key_b = window[:, :head_dim]
    value_b = window[:, head_dim:]
    visible = window_mask(query_b.shape[0], window.shape[0], positions)[None]
    scores = jnp.einsum("thd,kd->htk", query_b, key_b, preferred_element_type=jnp.float32)
    attn_prob = jnp.where(visible, jnp.exp(scores - log_total), 0.0)
    prob_b = attn_prob.astype(jnp.bfloat16)
    grad_prob = jnp.einsum("thd,kd->htk", grad_b, value_b, preferred_element_type=jnp.float32)
    row_dot = jnp.sum(attn_prob * grad_prob, axis=-1, keepdims=True)
    grad_score = (attn_prob * (grad_prob - row_dot)).astype(jnp.bfloat16)
    grad_query = jnp.einsum("htk,kd->thd", grad_score, key_b, preferred_element_type=jnp.float32)
    grad_key = jnp.einsum("htk,thd->kd", grad_score, query_b, preferred_element_type=jnp.float32)
    grad_value = jnp.einsum("htk,thd->kd", prob_b, grad_b, preferred_element_type=jnp.float32)
    return (grad_query, jnp.concatenate([grad_key, grad_value], axis=1))


def run_layer(
    tokens, cotangent, positions, attn_parts, fetch_ffn, send_ffn, send_attn, attend_rows, attend_back_rows
):
    w_q, w_k, w_v, w_o, g_in, g_q, g_k, g_mid = attn_parts
    gain_in = g_in.astype(jnp.float32)
    gain_q = g_q.astype(jnp.float32)
    gain_k = g_k.astype(jnp.float32)
    gain_mid = g_mid.astype(jnp.float32)
    row_count = tokens.shape[0]
    residual = tokens.astype(jnp.float32)
    normed, recip_in = norm_fwd(residual, gain_in)
    normed_b = normed.astype(jnp.bfloat16)
    queries = jnp.dot(normed_b, w_q, preferred_element_type=jnp.float32).reshape(row_count, H, HD)
    key_rows = jnp.dot(normed_b, w_k, preferred_element_type=jnp.float32)
    value_rows = jnp.dot(normed_b, w_v, preferred_element_type=jnp.float32)
    queries_n, recip_q = norm_fwd(queries, gain_q)
    keys_n, recip_k = norm_fwd(key_rows, gain_k)
    cosine, sine_t = rope_tables(positions)
    q_scale = HD ** (-0.5)
    query_b = (rotate(queries_n, cosine[:, None], sine_t[:, None]) * q_scale).astype(jnp.bfloat16)
    key_b = rotate(keys_n, cosine, sine_t).astype(jnp.bfloat16)
    kv_rows = jnp.concatenate([key_b, value_rows.astype(jnp.bfloat16)], axis=1)
    attended, kept_state = attend_rows(query_b, kv_rows, positions)
    attended_b = attended.reshape(row_count, H * HD).astype(jnp.bfloat16)
    branch = jnp.dot(attended_b, w_o, preferred_element_type=jnp.float32)
    branch_n, recip_mid = norm_fwd(branch, gain_mid)
    middle = residual + branch_n
    (w_g, w_u, w_d, g_pre, g_post), middle = fetch_ffn(middle)
    gain_pre = g_pre.astype(jnp.float32)
    gain_post = g_post.astype(jnp.float32)
    pre_n, recip_pre = norm_fwd(middle, gain_pre)
    pre_b = pre_n.astype(jnp.bfloat16)
    gate_v = jnp.dot(pre_b, w_g, preferred_element_type=jnp.float32)
    upper = jnp.dot(pre_b, w_u, preferred_element_type=jnp.float32)
    activated, slope_v = gelu_pair(gate_v)
    hidden_b = (activated * upper).astype(jnp.bfloat16)
    ffn_out = jnp.dot(hidden_b, w_d, preferred_element_type=jnp.float32)
    ffn_n, recip_post = norm_fwd(ffn_out, gain_post)
    output = (middle + ffn_n).astype(jnp.bfloat16)
    grad_top = cotangent.astype(jnp.float32)
    grad_ffn, grad_post = norm_bwd(ffn_out, recip_post, gain_post, grad_top)
    grad_ffn_b = grad_ffn.astype(jnp.bfloat16)
    grad_hidden = times_trans(grad_ffn_b, w_d)
    grad_gate_b = (grad_hidden * upper * slope_v).astype(jnp.bfloat16)
    grad_upper_b = (grad_hidden * activated).astype(jnp.bfloat16)
    grad_pre_in = times_trans(grad_gate_b, w_g) + times_trans(grad_upper_b, w_u)
    grad_mid_add, grad_pre = norm_bwd(middle, recip_pre, gain_pre, grad_pre_in)
    grad_middle = grad_top + grad_mid_add
    ffn_result = send_ffn(
        [pre_b, pre_b, hidden_b],
        [grad_gate_b, grad_upper_b, grad_ffn_b],
        jnp.concatenate([grad_pre, grad_post]).reshape(-1, 128),
    )
    grad_branch, grad_gmid = norm_bwd(branch, recip_mid, gain_mid, grad_middle)
    grad_branch_b = grad_branch.astype(jnp.bfloat16)
    grad_att_b = times_trans(grad_branch_b, w_o).reshape(row_count, H, HD).astype(jnp.bfloat16)
    grad_query, grad_kv = attend_back_rows(kept_state, grad_att_b)
    grad_qn = rotate_back(grad_query * q_scale, cosine[:, None], sine_t[:, None])
    grad_q, grad_gq = norm_bwd(queries, recip_q, gain_q, grad_qn)
    grad_kn = rotate_back(grad_kv[:, :HD], cosine, sine_t)
    grad_k, grad_gk = norm_bwd(key_rows, recip_k, gain_k, grad_kn)
    grad_q_b = grad_q.reshape(row_count, H * HD).astype(jnp.bfloat16)
    grad_k_b = grad_k.astype(jnp.bfloat16)
    grad_v_b = grad_kv[:, HD:].astype(jnp.bfloat16)
    grad_normed = (
        times_trans(grad_q_b, w_q) + times_trans(grad_k_b, w_k) + times_trans(grad_v_b, w_v)
    )
    grad_in_add, grad_gin = norm_bwd(residual, recip_in, gain_in, grad_normed)
    grad_tokens = grad_middle + grad_in_add
    attn_result = send_attn(
        [normed_b, normed_b, normed_b, attended_b],
        [grad_q_b, grad_k_b, grad_v_b, grad_branch_b],
        jnp.concatenate([grad_gin, grad_gq, grad_gk, grad_gmid]).reshape(-1, 128),
    )
    return (output, grad_tokens, attn_result, ffn_result)


def adam_step(param, grad_in, moment_one, moment_two):
    new_one = BETA_ONE * moment_one + (1.0 - BETA_ONE) * grad_in
    new_two = BETA_TWO * moment_two + (1.0 - BETA_TWO) * grad_in * grad_in
    corr_one = new_one / (1.0 - BETA_ONE**STEP)
    corr_two = new_two / (1.0 - BETA_TWO**STEP)
    new_param = param - LEARN_RATE * (
        corr_one / (jnp.sqrt(corr_two) + ADAM_EPS) + WEIGHT_DECAY * param
    )
    return (new_param, new_one, new_two)


def device_attend(query_b, kv_rows, positions):
    tok_rows = kv_rows.shape[0]
    reach = (WINDOW - 1) // tok_rows + 1
    pieces = []
    for shift_by in range(reach, 0, -1):
        pieces.append(passed_along(kv_rows, "group", shift_by))
    window = jnp.concatenate(pieces + [kv_rows], axis=0)
    attended, log_total = attend(query_b, window, positions)
    return (attended, (query_b, window, positions, log_total))


def device_attend_back(kept_state, grad_b):
    query_b, window, positions, log_total = kept_state
    grad_query, grad_window = attend_back(query_b, window, positions, log_total, grad_b)
    tok_rows = query_b.shape[0]
    reach = window.shape[0] // tok_rows - 1
    totals = grad_window[reach * tok_rows :]
    for shift_by in range(reach, 0, -1):
        slot_idx = reach - shift_by
        piece = grad_window[slot_idx * tok_rows : (slot_idx + 1) * tok_rows]
        totals = totals + passed_along(piece.astype(jnp.bfloat16), "group", -shift_by).astype(
            piece.dtype
        )
    return (grad_query, totals)


BF = jnp.bfloat16
F32 = jnp.float32
VMEM_LIMIT = 60 * 1024 * 1024


def rows_up(count, unit=16):
    return -(-count // unit) * unit


def pack_body(jobs, own, padded, sizes, core_ref, *refs):
    count = len(jobs)
    lefts, rights, gains = refs[:count], refs[count : 2 * count], refs[2 * count]
    send_ref, keep_ref, flat = refs[2 * count + 1 :]
    offset = 0
    tile = 128
    for (m, n), left, right in zip(jobs, lefts, rights):
        per_row = n // 128

        def step(i, carry, left=left, right=right, per_row=per_row, offset=offset):
            start = pl.multiple_of(i * tile, tile)
            block = lax.dot_general(
                left[:, pl.ds(start, tile)],
                right[...],
                (((0,), (0,)), ((), ())),
                preferred_element_type=F32,
            )
            base = offset + i * (tile * per_row)
            for j in range(per_row):
                flat[pl.ds(base + j, tile, stride=per_row), :] = block[:, 128 * j : 128 * j + 128]
            return carry

        lax.fori_loop(0, m // tile, step, 0)
        offset = offset + m * per_row
    tail = flat.shape[0] - offset
    flat[pl.ds(offset, tail), :] = jnp.zeros((tail, 128), F32)
    flat[pl.ds(offset, gains.shape[0]), :] = gains[...]
    slow, fast, cores, depth = sizes
    half = slow * fast * depth
    core = core_ref[0]

    def cut(i, carry):
        lead, z = i // depth, i % depth
        mine = ((lead * 2 + core) * depth + z) * own
        other = ((lead * 2 + 1 - core) * depth + z) * own
        keep_ref[i] = flat[pl.ds(mine, padded), :].astype(BF)
        send_ref[i] = flat[pl.ds(other, padded), :].astype(BF)
        return carry

    lax.fori_loop(0, half, cut, 0)


def pack_grads(jobs, lefts, rights, gains, own, sizes, core):
    padded = rows_up(own)
    devices = math.prod(sizes)
    half = devices // 2
    whole = rows_up(devices * own + 16, 8)
    out = jax.ShapeDtypeStruct((half, padded, 128), BF)
    vmem = pl.BlockSpec(memory_space=pltpu.VMEM)
    flops = sum(2 * m * n * lefts[0].shape[0] for m, n in jobs)
    return pl.pallas_call(
        functools.partial(pack_body, jobs, own, padded, sizes),
        out_shape=(out, out),
        in_specs=[pl.BlockSpec(memory_space=pltpu.SMEM)] + [vmem] * (2 * len(jobs) + 1),
        out_specs=(vmem, vmem),
        scratch_shapes=[pltpu.VMEM((whole, 128), F32)],
        compiler_params=pltpu.CompilerParams(vmem_limit_bytes=VMEM_LIMIT),
        cost_estimate=pl.CostEstimate(
            flops=flops, bytes_accessed=devices * padded * 256, transcendentals=0
        ),
    )(core, *lefts, *rights, gains)


def spread(flat, dims_list, outs):
    offset = 0
    tile = 128
    for (m, n), out in zip(dims_list, outs):
        per_row = n // 128

        def step(i, carry, out=out, per_row=per_row, offset=offset):
            start = pl.multiple_of(i * tile, tile)
            base = offset + i * (tile * per_row)
            for j in range(per_row):
                piece = flat[pl.ds(base + j, tile, stride=per_row), :]
                out[pl.ds(start, tile), 128 * j : 128 * j + 128] = piece.astype(BF)
            return carry

        lax.fori_loop(0, m // tile, step, 0)
        offset = offset + m * per_row
    outs[-1][...] = flat[pl.ds(offset, outs[-1].shape[0]), :]


def unpack_whole_body(dims_list, own, blocks, *refs):
    outs, flat = refs[:-1], refs[-1]

    def put(d, carry):
        flat[pl.ds(d * own, own), :] = blocks[d].astype(F32)
        return carry

    lax.fori_loop(0, blocks.shape[0], put, 0)
    spread(flat, dims_list, outs)


def unpack_pieces_body(dims_list, own, sizes, at_ref, *refs):
    first, first_far, second, second_far = refs[:4]
    outs, flat = refs[4:-1], refs[-1]
    slow, fast, cores, depth = sizes
    head = first.shape[1]
    near = tuple(at_ref[i] for i in range(3))

    def seen(extent, owner, here):
        return owner ^ here if extent == 2 else owner

    def put(i, carry):
        z, b, a = i % depth, (i // depth) % fast, i // (depth * fast)
        ra, rb = seen(slow, a, near[0]), seen(fast, b, near[1])
        one = (ra * fast + rb) * depth + z
        two = (rb * slow + ra) * depth + z
        for core, left, right in ((near[2], first, second), (1 - near[2], first_far, second_far)):
            base = (((a * fast + b) * 2 + core) * depth + z) * own
            flat[pl.ds(base, head), :] = left[one].astype(F32)
            flat[pl.ds(base + head, own - head), :] = right[two, : own - head].astype(F32)
        return carry

    lax.fori_loop(0, slow * fast * depth, put, 0)
    spread(flat, dims_list, outs)


def unpack(body, dims_list, gain_rows, own, devices, ins, scalars=()):
    vmem = pl.BlockSpec(memory_space=pltpu.VMEM)
    outs = [jax.ShapeDtypeStruct(dims, BF) for dims in dims_list]
    outs.append(jax.ShapeDtypeStruct((rows_up(gain_rows, 8), 128), F32))
    return pl.pallas_call(
        body,
        out_shape=tuple(outs),
        in_specs=[pl.BlockSpec(memory_space=pltpu.SMEM)] * len(scalars) + [vmem] * len(ins),
        out_specs=tuple([vmem] * len(outs)),
        scratch_shapes=[pltpu.VMEM((rows_up(devices * own + 8, 8), 128), F32)],
        compiler_params=pltpu.CompilerParams(vmem_limit_bytes=VMEM_LIMIT),
        cost_estimate=pl.CostEstimate(
            flops=0, bytes_accessed=devices * own * 512, transcendentals=0
        ),
    )(*scalars, *ins)


def cut_gains(rows, lengths):
    line = rows.reshape(-1)
    starts = [sum(lengths[:i]) for i in range(len(lengths))]
    return tuple(line[a : a + b] for a, b in zip(starts, lengths))


def grid_of():
    pairs = lax.axis_size("dp") // 2
    slow = math.isqrt(pairs)
    fast = pairs // slow
    depth = lax.axis_size("group")
    place = lax.axis_index("dp")
    where = (place // (2 * fast), (place // 2) % fast, place % 2, lax.axis_index("group"))
    return ((slow, fast, 2, depth), where)


def step_along(value, axis, by, sizes, senders=None):
    extent = sizes[axis]
    pairs = []
    if axis == 3:
        for i in range(extent):
            if 0 <= i + by < extent and (senders is None or i in senders):
                pairs.append((i, i + by))
        return lax.ppermute(value, "group", pairs)
    stride = (2 * sizes[1], 2, 1)[axis]
    for i in range(sizes[0] * sizes[1] * 2):
        at = (i // stride) % extent
        if 0 <= at + by < extent and (senders is None or at in senders):
            pairs.append((i, i + by * stride))
    return lax.ppermute(value, "dp", pairs)


def swap_along(value, axis, sizes):
    stride = (2 * sizes[1], 2, 1)[axis]
    count = sizes[0] * sizes[1] * 2
    pairs = [(i, i + stride * (1 - 2 * ((i // stride) % 2))) for i in range(count)]
    return lax.ppermute(value, "dp", pairs)


def gather_axis(value, axis, sizes):
    extent = sizes[axis]
    if extent == 2:
        return jnp.stack([value, swap_along(value, axis, sizes)])
    stride = (2 * sizes[1], 2, 1)[axis]
    count = sizes[0] * sizes[1] * 2
    groups = [
        [i + k * stride for k in range(extent)] for i in range(count) if (i // stride) % extent == 0
    ]
    return lax.all_gather(value, "dp", axis=0, axis_index_groups=groups)


def gather_pieces(block, sizes):
    head = block.shape[0] // 32 * 16
    line = lax.all_gather(block, "group", axis=0)
    pieces = []
    for part, order in ((line[:, :head], (1, 0)), (line[:, head:], (0, 1))):
        for axis in order:
            part = gather_axis(part, axis, sizes)
        part = part.reshape(-1, *part.shape[-2:])
        pieces += [part, swap_along(part, 2, sizes)]
    return pieces


def pick(blocks, index):
    return lax.dynamic_index_in_dim(blocks, index, axis=0, keepdims=False)


def scatter_axis(blocks, axis, sizes, where):
    extent, at = (sizes[axis], where[axis])
    if extent == 1:
        return blocks[0].astype(jnp.float32)
    if extent == 2 and axis < 3:
        arrived = swap_along(pick(blocks, 1 - at), axis, sizes)
        return pick(blocks, at).astype(jnp.float32) + arrived.astype(jnp.float32)
    total = pick(blocks, at).astype(jnp.float32)
    for by in (1, -1):
        arrived = None
        for step in range(1, extent):
            dest = jnp.clip(at + by * (extent - step), 0, extent - 1)
            load = pick(blocks, dest)
            if arrived is not None:
                load = (load.astype(jnp.float32) + arrived.astype(jnp.float32)).astype(jnp.bfloat16)
            senders = range(step) if by == 1 else range(extent - step, extent)
            arrived = step_along(load, axis, by, sizes, senders)
        total = total + arrived.astype(jnp.float32)
    return total


def after_core(pair, sizes):
    send, keep = pair
    arrived = swap_along(send, 2, sizes)
    total = (keep.astype(F32) + arrived.astype(F32)).astype(BF)
    return total.reshape(sizes[0], sizes[1], sizes[3], *send.shape[1:])


def scatter_sum(pair, sizes, where):
    held = after_core(pair, sizes)
    cut = held.shape[3] // 32 * 16
    first = held[:, :, :, :cut]
    second = held[:, :, :, cut:].transpose(1, 0, 2, 3, 4)
    first = scatter_axis(first, 0, sizes, where).astype(BF)
    second = scatter_axis(second, 1, sizes, where).astype(BF)
    first = scatter_axis(first, 1, sizes, where).astype(BF)
    second = scatter_axis(second, 0, sizes, where).astype(BF)
    return scatter_axis(jnp.concatenate([first, second], axis=1), 3, sizes, where)


def shards(tokens, cotangent, positions, attn_weights, ffn_weights, attn_m, attn_v, ffn_m, ffn_v):
    sizes, where = grid_of()
    core = where[2].astype(jnp.int32).reshape(1)
    attn_own, ffn_own = (attn_weights.shape[0], ffn_weights.shape[0])

    devices = math.prod(sizes)
    ffn_full = lax.all_gather(ffn_weights.astype(BF), ("dp", "group"), axis=0)
    block = jnp.pad(attn_weights.astype(BF), ((0, rows_up(attn_own) - attn_own), (0, 0)))
    dims = attn_shapes()[:4]
    attn_parts = unpack(
        functools.partial(unpack_pieces_body, dims, attn_own, sizes),
        dims,
        14,
        attn_own,
        devices,
        gather_pieces(block, sizes),
        (jnp.stack(where[:3]).astype(jnp.int32),),
    )
    attn_parts = attn_parts[:4] + cut_gains(attn_parts[4], (D, HD, HD, D))

    def fetch_ffn(middle):
        full, middle = lax.optimization_barrier((ffn_full, middle))
        dims = ffn_shapes()[:3]
        parts = unpack(
            functools.partial(unpack_whole_body, dims, ffn_own), dims, 10, ffn_own, devices, [full]
        )
        return parts[:3] + cut_gains(parts[3], (D, D)), middle

    def send_ffn(lefts, rights, gains):
        return pack_grads(ffn_shapes()[:3], lefts, rights, gains, ffn_own, sizes, core)

    def send_attn(lefts, rights, gains):
        return pack_grads(attn_shapes()[:4], lefts, rights, gains, attn_own, sizes, core)

    output, grad_tokens, attn_result, ffn_result = run_layer(
        tokens,
        cotangent,
        positions,
        attn_parts,
        fetch_ffn,
        send_ffn,
        send_attn,
        device_attend,
        device_attend_back,
    )
    ffn_grad = scatter_sum(ffn_result, sizes, where)[:ffn_own]
    attn_grad = scatter_sum(attn_result, sizes, where)[:attn_own]
    attn_new, attn_m_new, attn_v_new = adam_step(attn_weights, attn_grad, attn_m, attn_v)
    ffn_new, ffn_m_new, ffn_v_new = adam_step(ffn_weights, ffn_grad, ffn_m, ffn_v)
    return (
        output,
        grad_tokens,
        attn_grad,
        ffn_grad,
        attn_new,
        ffn_new,
        attn_m_new,
        attn_v_new,
        ffn_m_new,
        ffn_v_new,
    )


def solution(mesh):
    placed = (
        P(("dp", "group"), None),
        P(("dp", "group"), None),
        P(("dp", "group")),
        P(("dp", "group"), None),
        P(("dp", "group"), None),
        P(("dp", "group"), None),
        P(("dp", "group"), None),
        P(("dp", "group"), None),
        P(("dp", "group"), None),
    )
    return jax.shard_map(
        shards,
        mesh=mesh,
        in_specs=placed,
        out_specs=(
            P(("dp", "group"), None),
            P(("dp", "group"), None),
            P(("dp", "group"), None),
            P(("dp", "group"), None),
            P(("dp", "group"), None),
            P(("dp", "group"), None),
            P(("dp", "group"), None),
            P(("dp", "group"), None),
            P(("dp", "group"), None),
            P(("dp", "group"), None),
        ),
        check_vma=False,
    )
```

```python
import functools
import math

import jax
import jax.numpy as jnp
from jax import lax
from jax.experimental import pallas as pl
from jax.experimental.pallas import tpu as pltpu
from jax.sharding import PartitionSpec as P

D = 640
H = 4
HD = 256
FF = 2048
WINDOW = 512
STEP = 3


NORM_EPS = 1e-06
THETA = 10000.0
BETA_ONE = 0.9
BETA_TWO = 0.95
LEARN_RATE = 0.02
WEIGHT_DECAY = 0.1
ADAM_EPS = 1e-08
GELU_COEF = 0.7978845608028654


def passed_along(shard, axis, by):
    count = lax.axis_size(axis)
    pairs = [(i, i + by) for i in range(count) if 0 <= i + by < count]
    return lax.ppermute(shard, axis, pairs)


def attn_shapes():
    return [(D, H * HD), (D, HD), (D, HD), (H * HD, D), (D,), (HD,), (HD,), (D,)]


def ffn_shapes():
    return [(D, FF), (D, FF), (FF, D), (D,), (D,)]


def rope_tables(positions):
    half_dim = HD // 2
    freqs = jnp.power(THETA, -2.0 * jnp.arange(half_dim, dtype=jnp.float32) / HD)
    angles = positions.astype(jnp.float32)[:, None] * freqs[None, :]
    return (jnp.cos(angles), jnp.sin(angles))


def gelu_pair(values):
    tangent = jnp.tanh(GELU_COEF * (values + 0.044715 * (values * values * values)))
    activated = 0.5 * values * (1.0 + tangent)
    slope_v = 0.5 * (1.0 + tangent) + 0.5 * values * (1.0 - tangent * tangent) * GELU_COEF * (
        1.0 + 3.0 * 0.044715 * values * values
    )
    return (activated, slope_v)


def times_trans(left, right):
    return lax.dot_general(
        left, right, (((1,), (1,)), ((), ())), preferred_element_type=jnp.float32
    )


def adam_step(param, grad_in, moment_one, moment_two):
    new_one = BETA_ONE * moment_one + (1.0 - BETA_ONE) * grad_in
    new_two = BETA_TWO * moment_two + (1.0 - BETA_TWO) * grad_in * grad_in
    corr_one = new_one / (1.0 - BETA_ONE**STEP)
    corr_two = new_two / (1.0 - BETA_TWO**STEP)
    new_param = param - LEARN_RATE * (
        corr_one / (jnp.sqrt(corr_two) + ADAM_EPS) + WEIGHT_DECAY * param
    )
    return (new_param, new_one, new_two)


BF = jnp.bfloat16
F32 = jnp.float32
VMEM_LIMIT = 60 * 1024 * 1024


def rows_up(count, unit=16):
    return -(-count // unit) * unit


def pack_body(jobs, own, padded, sizes, core_ref, *refs):
    count = len(jobs)
    lefts, rights, gains = refs[:count], refs[count : 2 * count], refs[2 * count]
    send_ref, keep_ref, flat = refs[2 * count + 1 :]
    offset = 0
    tile = 128
    for (m, n), left, right in zip(jobs, lefts, rights):
        per_row = n // 128

        def step(i, carry, left=left, right=right, per_row=per_row, offset=offset):
            start = pl.multiple_of(i * tile, tile)
            block = lax.dot_general(
                left[:, pl.ds(start, tile)],
                right[...],
                (((0,), (0,)), ((), ())),
                preferred_element_type=F32,
            )
            base = offset + i * (tile * per_row)
            for j in range(per_row):
                flat[pl.ds(base + j, tile, stride=per_row), :] = block[:, 128 * j : 128 * j + 128]
            return carry

        lax.fori_loop(0, m // tile, step, 0)
        offset = offset + m * per_row
    tail = flat.shape[0] - offset
    flat[pl.ds(offset, tail), :] = jnp.zeros((tail, 128), F32)
    flat[pl.ds(offset, gains.shape[0]), :] = gains[...]
    slow, fast, cores, depth = sizes
    half = slow * fast * depth
    core = core_ref[0]

    def cut(i, carry):
        lead, z = i // depth, i % depth
        mine = ((lead * 2 + core) * depth + z) * own
        other = ((lead * 2 + 1 - core) * depth + z) * own
        keep_ref[i] = flat[pl.ds(mine, padded), :].astype(BF)
        send_ref[i] = flat[pl.ds(other, padded), :].astype(BF)
        return carry

    lax.fori_loop(0, half, cut, 0)


def pack_grads(jobs, lefts, rights, gains, own, sizes, core):
    padded = rows_up(own)
    devices = math.prod(sizes)
    half = devices // 2
    whole = rows_up(devices * own + 16, 8)
    out = jax.ShapeDtypeStruct((half, padded, 128), BF)
    vmem = pl.BlockSpec(memory_space=pltpu.VMEM)
    flops = sum(2 * m * n * lefts[0].shape[0] for m, n in jobs)
    return pl.pallas_call(
        functools.partial(pack_body, jobs, own, padded, sizes),
        out_shape=(out, out),
        in_specs=[pl.BlockSpec(memory_space=pltpu.SMEM)] + [vmem] * (2 * len(jobs) + 1),
        out_specs=(vmem, vmem),
        scratch_shapes=[pltpu.VMEM((whole, 128), F32)],
        compiler_params=pltpu.CompilerParams(vmem_limit_bytes=VMEM_LIMIT),
        cost_estimate=pl.CostEstimate(
            flops=flops, bytes_accessed=devices * padded * 256, transcendentals=0
        ),
    )(core, *lefts, *rights, gains)


def spread(flat, dims_list, outs):
    offset = 0
    tile = 128
    for (m, n), out in zip(dims_list, outs):
        per_row = n // 128

        def step(i, carry, out=out, per_row=per_row, offset=offset):
            start = pl.multiple_of(i * tile, tile)
            base = offset + i * (tile * per_row)
            for j in range(per_row):
                piece = flat[pl.ds(base + j, tile, stride=per_row), :]
                out[pl.ds(start, tile), 128 * j : 128 * j + 128] = piece.astype(BF)
            return carry

        lax.fori_loop(0, m // tile, step, 0)
        offset = offset + m * per_row
    outs[-1][...] = flat[pl.ds(offset, outs[-1].shape[0]), :]


def unpack_whole_body(dims_list, own, blocks, *refs):
    outs, flat = refs[:-1], refs[-1]

    def put(d, carry):
        flat[pl.ds(d * own, own), :] = blocks[d].astype(F32)
        return carry

    lax.fori_loop(0, blocks.shape[0], put, 0)
    spread(flat, dims_list, outs)


def unpack_pieces_body(dims_list, own, sizes, at_ref, *refs):
    first, first_far, second, second_far = refs[:4]
    outs, flat = refs[4:-1], refs[-1]
    slow, fast, cores, depth = sizes
    head = first.shape[1]
    near = tuple(at_ref[i] for i in range(3))

    def seen(extent, owner, here):
        return owner ^ here if extent == 2 else owner

    def put(i, carry):
        z, b, a = i % depth, (i // depth) % fast, i // (depth * fast)
        ra, rb = seen(slow, a, near[0]), seen(fast, b, near[1])
        one = (ra * fast + rb) * depth + z
        two = (rb * slow + ra) * depth + z
        for core, left, right in ((near[2], first, second), (1 - near[2], first_far, second_far)):
            base = (((a * fast + b) * 2 + core) * depth + z) * own
            flat[pl.ds(base, head), :] = left[one].astype(F32)
            flat[pl.ds(base + head, own - head), :] = right[two, : own - head].astype(F32)
        return carry

    lax.fori_loop(0, slow * fast * depth, put, 0)
    spread(flat, dims_list, outs)


def unpack(body, dims_list, gain_rows, own, devices, ins, scalars=()):
    vmem = pl.BlockSpec(memory_space=pltpu.VMEM)
    outs = [jax.ShapeDtypeStruct(dims, BF) for dims in dims_list]
    outs.append(jax.ShapeDtypeStruct((rows_up(gain_rows, 8), 128), F32))
    return pl.pallas_call(
        body,
        out_shape=tuple(outs),
        in_specs=[pl.BlockSpec(memory_space=pltpu.SMEM)] * len(scalars) + [vmem] * len(ins),
        out_specs=tuple([vmem] * len(outs)),
        scratch_shapes=[pltpu.VMEM((rows_up(devices * own + 8, 8), 128), F32)],
        compiler_params=pltpu.CompilerParams(vmem_limit_bytes=VMEM_LIMIT),
        cost_estimate=pl.CostEstimate(
            flops=0, bytes_accessed=devices * own * 512, transcendentals=0
        ),
    )(*scalars, *ins)


def contract(left, right, left_dim, right_dim):
    return lax.dot_general(
        left, right, (((left_dim,), (right_dim,)), ((), ())), preferred_element_type=F32
    )


def row_norm(values):
    return lax.rsqrt(jnp.mean(values * values, axis=-1, keepdims=True) + NORM_EPS)


def turn(values, cosine, sine_t, sign):
    first, second = values[:, : HD // 2], values[:, HD // 2 :]
    return jnp.concatenate(
        [first * cosine - sign * (second * sine_t), second * cosine + sign * (first * sine_t)],
        axis=-1,
    )


def seen_keys(reach, place, own, window):
    gap = lax.broadcasted_iota(jnp.int32, (own, window), 0) + (window - own)
    gap = gap - lax.broadcasted_iota(jnp.int32, (own, window), 1)
    return (gap >= 0) & (gap <= jnp.minimum(place, reach - 1))


def norm_grad(values, recip, gain, grad_out):
    scaled = grad_out * (1.0 + gain)
    grad_in = recip * scaled - values * recip * recip * recip * jnp.mean(
        scaled * values, axis=-1, keepdims=True
    )
    return grad_in, jnp.sum(grad_out * values * recip, axis=0, keepdims=True)


def attention_body(
    tokens, place, cosine, sine_t, w_q, w_k, w_v, w_o, g_in, g_q, g_k, g_mid,
    normed_b, queries, keys, query_b, key_b, value_b, attended_b, branch, middle,
):
    window, own = tokens.shape[0], place.shape[0]
    start = window - own
    values = tokens[...].astype(F32)
    normed_b[...] = (values * row_norm(values) * (1.0 + g_in[...])).astype(BF)
    keys[...] = contract(normed_b[...], w_k[...], 1, 0)
    value_b[...] = contract(normed_b[...], w_v[...], 1, 0).astype(BF)
    keyed = keys[...]
    keyed = keyed * row_norm(keyed) * (1.0 + g_k[...])
    key_b[...] = turn(keyed, cosine[...], sine_t[...], 1.0).astype(BF)
    queries[...] = contract(normed_b[start:, :], w_q[...], 1, 0)

    def head(h, carry):
        at = pl.ds(pl.multiple_of(h * HD, HD), HD)
        asked = queries[:, at]
        asked = asked * row_norm(asked) * (1.0 + g_q[...])
        asked = turn(asked, cosine[start:, :], sine_t[start:, :], 1.0) * (HD ** (-0.5))
        query_b[:, at] = asked.astype(BF)
        visible = seen_keys(WINDOW, place[...], own, window)
        scores = contract(query_b[:, at], key_b[...], 1, 1)
        total = jnp.sum(jnp.where(visible, jnp.exp(scores), 0.0), axis=-1, keepdims=True)
        prob = jnp.where(visible, jnp.exp(scores - jnp.log(total)), 0.0)
        attended_b[:, at] = contract(prob.astype(BF), value_b[...], 1, 0).astype(BF)
        return carry

    lax.fori_loop(0, H, head, 0)
    branch[...] = contract(attended_b[...], w_o[...], 1, 0)
    out = branch[...]
    middle[...] = values[start:, :] + out * row_norm(out) * (1.0 + g_mid[...])


def attention_back_body(
    grad_middle, branch, tokens, place, cosine, sine_t, queries, keys, query_b, key_b, value_b,
    w_q, w_k, w_v, w_o, g_in, g_q, g_k, g_mid,
    grad_branch_b, grad_q_b, grad_k_b, grad_v_b, grad_normed, sum_in, sum_q, sum_k, sum_mid,
    grad_key, grad_value,
):
    window, own = tokens.shape[0], place.shape[0]
    start = window - own
    out = branch[...]
    grad_branch, sum_mid[...] = norm_grad(out, row_norm(out), g_mid[...], grad_middle[...])
    grad_branch_b[...] = grad_branch.astype(BF)
    grad_key[...] = jnp.zeros_like(grad_key)
    grad_value[...] = jnp.zeros_like(grad_value)
    sum_q[...] = jnp.zeros_like(sum_q)

    def head(h, carry):
        at = pl.ds(pl.multiple_of(h * HD, HD), HD)
        grad_att = contract(grad_branch_b[...], w_o[at, :], 1, 1).astype(BF)
        visible = seen_keys(WINDOW, place[...], own, window)
        scores = contract(query_b[:, at], key_b[...], 1, 1)
        total = jnp.sum(jnp.where(visible, jnp.exp(scores), 0.0), axis=-1, keepdims=True)
        prob = jnp.where(visible, jnp.exp(scores - jnp.log(total)), 0.0)
        grad_prob = contract(grad_att, value_b[...], 1, 1)
        row_dot = jnp.sum(prob * grad_prob, axis=-1, keepdims=True)
        grad_score = (prob * (grad_prob - row_dot)).astype(BF)
        grad_query = contract(grad_score, key_b[...], 1, 0)
        grad_key[...] += contract(grad_score, query_b[:, at], 0, 0)
        grad_value[...] += contract(prob.astype(BF), grad_att, 0, 0)
        back = turn(grad_query * (HD ** (-0.5)), cosine[start:, :], sine_t[start:, :], -1.0)
        asked = queries[:, at]
        grad_q, part = norm_grad(asked, row_norm(asked), g_q[...], back)
        grad_q_b[:, at] = grad_q.astype(BF)
        sum_q[...] += part
        return carry

    lax.fori_loop(0, H, head, 0)
    keyed = keys[...]
    back = turn(grad_key[...], cosine[...], sine_t[...], -1.0)
    grad_k, sum_k[...] = norm_grad(keyed, row_norm(keyed), g_k[...], back)
    grad_k_b[...] = grad_k.astype(BF)
    grad_v_b[...] = grad_value[...].astype(BF)
    grad_normed[...] = contract(grad_q_b[...], w_q[...], 1, 1)
    through = contract(grad_k_b[...], w_k[...], 1, 1) + contract(grad_v_b[...], w_v[...], 1, 1)
    values = tokens[...].astype(F32)
    scaled = values * row_norm(values)
    sum_in[...] = jnp.sum(through * scaled, axis=0, keepdims=True) + jnp.sum(
        grad_normed[...] * scaled[start:, :], axis=0, keepdims=True
    )


def in_vmem(body, outs, scratch, flops, args):
    vmem = pl.BlockSpec(memory_space=pltpu.VMEM)
    out_shape = tuple(jax.ShapeDtypeStruct(shape, kind) for shape, kind in outs)
    moved = sum(math.prod(o.shape) * o.dtype.itemsize for o in (*out_shape, *args))
    return pl.pallas_call(
        body,
        out_shape=out_shape,
        in_specs=[vmem] * len(args),
        out_specs=tuple([vmem] * len(outs)),
        scratch_shapes=[pltpu.VMEM(shape, F32) for shape in scratch],
        compiler_params=pltpu.CompilerParams(vmem_limit_bytes=VMEM_LIMIT),
        cost_estimate=pl.CostEstimate(flops=flops, bytes_accessed=moved, transcendentals=0),
    )(*args)


def attention(tokens, place, cosine, sine_t, weights):
    window, own = tokens.shape[0], place.shape[0]
    outs = [
        ((window, D), BF), ((own, H * HD), F32), ((window, HD), F32), ((own, H * HD), BF),
        ((window, HD), BF), ((window, HD), BF), ((own, H * HD), BF), ((own, D), F32), ((own, D), F32),
    ]
    flops = 4 * own * window * H * HD + 4 * own * D * H * HD + 4 * window * D * HD
    return in_vmem(attention_body, outs, (), flops, (tokens, place, cosine, sine_t, *weights))


def attention_back(grad_middle, branch, tokens, place, cosine, sine_t, kept, weights):
    window, own = tokens.shape[0], place.shape[0]
    outs = [
        ((own, D), BF), ((own, H * HD), BF), ((window, HD), BF), ((window, HD), BF), ((own, D), F32),
        ((1, D), F32), ((1, HD), F32), ((1, HD), F32), ((1, D), F32),
    ]
    flops = 10 * own * window * H * HD + 4 * own * D * H * HD + 4 * window * D * HD
    args = (grad_middle, branch, tokens, place, cosine, sine_t, *kept, *weights)
    return in_vmem(attention_back_body, outs, ((window, HD), (window, HD)), flops, args)


def feed_forward_body(
    middle, top_in, w_g, w_u, w_d, g_pre, g_post,
    output, pre_b, hidden_b, grad_ffn_b, grad_gate_b, grad_upper_b, grad_middle, sum_pre, sum_post,
    gate, upper, total,
):
    tile = 512
    steps = gate.shape[1] // tile
    values = middle[...]
    recip = row_norm(values)
    pre_b[...] = (values * recip * (1.0 + g_pre[...])).astype(BF)
    total[...] = jnp.zeros_like(total)

    def forward(t, carry):
        at = pl.ds(pl.multiple_of(t * tile, tile), tile)
        gate_t = contract(pre_b[...], w_g[:, at], 1, 0)
        upper_t = contract(pre_b[...], w_u[:, at], 1, 0)
        gate[:, at] = gate_t
        upper[:, at] = upper_t
        activated, _ = gelu_pair(gate_t)
        hidden_b[:, at] = (activated * upper_t).astype(BF)
        total[...] += contract(hidden_b[:, at], w_d[at, :], 1, 0)
        return carry

    lax.fori_loop(0, steps, forward, 0)
    ffn_out = total[...]
    recip_post = row_norm(ffn_out)
    output[...] = (values + ffn_out * recip_post * (1.0 + g_post[...])).astype(BF)
    top = top_in[...].astype(F32)
    grad_ffn, sum_post[...] = norm_grad(ffn_out, recip_post, g_post[...], top)
    grad_ffn_b[...] = grad_ffn.astype(BF)
    total[...] = jnp.zeros_like(total)

    def backward(t, carry):
        at = pl.ds(pl.multiple_of(t * tile, tile), tile)
        grad_hidden = contract(grad_ffn_b[...], w_d[at, :], 1, 1)
        activated, slope = gelu_pair(gate[:, at])
        grad_gate_b[:, at] = (grad_hidden * upper[:, at] * slope).astype(BF)
        grad_upper_b[:, at] = (grad_hidden * activated).astype(BF)
        total[...] += contract(grad_gate_b[:, at], w_g[:, at], 1, 1)
        total[...] += contract(grad_upper_b[:, at], w_u[:, at], 1, 1)
        return carry

    lax.fori_loop(0, steps, backward, 0)
    grad_add, sum_pre[...] = norm_grad(values, recip, g_pre[...], total[...])
    grad_middle[...] = top + grad_add


def feed_forward(middle, cotangent, weights):
    own = middle.shape[0]
    outs = [
        ((own, D), BF), ((own, D), BF), ((own, FF), BF), ((own, D), BF), ((own, FF), BF),
        ((own, FF), BF), ((own, D), F32), ((1, D), F32), ((1, D), F32),
    ]
    scratch = ((own, FF), (own, FF), (own, D))
    return in_vmem(
        feed_forward_body, outs, scratch, 12 * own * D * FF, (middle, cotangent, *weights)
    )


def cut_gains(rows, lengths):
    line = rows.reshape(-1)
    starts = [sum(lengths[:i]) for i in range(len(lengths))]
    return tuple(line[a : a + b].reshape(1, b) for a, b in zip(starts, lengths))


def grid_of():
    pairs = lax.axis_size("dp") // 2
    slow = math.isqrt(pairs)
    fast = pairs // slow
    depth = lax.axis_size("group")
    place = lax.axis_index("dp")
    where = (place // (2 * fast), (place // 2) % fast, place % 2, lax.axis_index("group"))
    return ((slow, fast, 2, depth), where)


def step_along(value, axis, by, sizes, senders=None):
    extent = sizes[axis]
    pairs = []
    if axis == 3:
        for i in range(extent):
            if 0 <= i + by < extent and (senders is None or i in senders):
                pairs.append((i, i + by))
        return lax.ppermute(value, "group", pairs)
    stride = (2 * sizes[1], 2, 1)[axis]
    for i in range(sizes[0] * sizes[1] * 2):
        at = (i // stride) % extent
        if 0 <= at + by < extent and (senders is None or at in senders):
            pairs.append((i, i + by * stride))
    return lax.ppermute(value, "dp", pairs)


def swap_along(value, axis, sizes):
    stride = (2 * sizes[1], 2, 1)[axis]
    count = sizes[0] * sizes[1] * 2
    pairs = [(i, i + stride * (1 - 2 * ((i // stride) % 2))) for i in range(count)]
    return lax.ppermute(value, "dp", pairs)


def gather_axis(value, axis, sizes):
    extent = sizes[axis]
    if extent == 2:
        return jnp.stack([value, swap_along(value, axis, sizes)])
    stride = (2 * sizes[1], 2, 1)[axis]
    count = sizes[0] * sizes[1] * 2
    groups = [
        [i + k * stride for k in range(extent)] for i in range(count) if (i // stride) % extent == 0
    ]
    return lax.all_gather(value, "dp", axis=0, axis_index_groups=groups)


def gather_pieces(block, sizes):
    head = block.shape[0] // 32 * 16
    line = lax.all_gather(block, "group", axis=0)
    pieces = []
    for part, order in ((line[:, :head], (1, 0)), (line[:, head:], (0, 1))):
        for axis in order:
            part = gather_axis(part, axis, sizes)
        part = part.reshape(-1, *part.shape[-2:])
        pieces += [part, swap_along(part, 2, sizes)]
    return pieces


def pick(blocks, index):
    return lax.dynamic_index_in_dim(blocks, index, axis=0, keepdims=False)


def scatter_axis(blocks, axis, sizes, where):
    extent, at = (sizes[axis], where[axis])
    if extent == 1:
        return blocks[0].astype(jnp.float32)
    if extent == 2 and axis < 3:
        arrived = swap_along(pick(blocks, 1 - at), axis, sizes)
        return pick(blocks, at).astype(jnp.float32) + arrived.astype(jnp.float32)
    total = pick(blocks, at).astype(jnp.float32)
    for by in (1, -1):
        arrived = None
        for step in range(1, extent):
            dest = jnp.clip(at + by * (extent - step), 0, extent - 1)
            load = pick(blocks, dest)
            if arrived is not None:
                load = (load.astype(jnp.float32) + arrived.astype(jnp.float32)).astype(jnp.bfloat16)
            senders = range(step) if by == 1 else range(extent - step, extent)
            arrived = step_along(load, axis, by, sizes, senders)
        total = total + arrived.astype(jnp.float32)
    return total


def after_core(pair, sizes):
    send, keep = pair
    arrived = swap_along(send, 2, sizes)
    total = (keep.astype(F32) + arrived.astype(F32)).astype(BF)
    return total.reshape(sizes[0], sizes[1], sizes[3], *send.shape[1:])


class Summing:
    def __init__(self, pair, sizes, where):
        held = after_core(pair, sizes)
        cut = held.shape[3] // 32 * 16
        self.sizes, self.where = sizes, where
        self.first = held[:, :, :, :cut]
        self.second = held[:, :, :, cut:].transpose(1, 0, 2, 3, 4)
        self.axes = (0, 1)

    def load(self):
        if self.sizes[0] != 2 or self.sizes[1] != 2:
            return ()
        near, far = self.axes
        return (pick(self.first, 1 - self.where[near]), pick(self.second, 1 - self.where[far]))

    def move(self, loads):
        if not loads:
            near, far = self.axes
            one = scatter_axis(self.first, near, self.sizes, self.where)
            two = scatter_axis(self.second, far, self.sizes, self.where)
            self.sums = (one, two)
            return ()
        return tuple(swap_along(load, axis, self.sizes) for load, axis in zip(loads, self.axes))

    def add(self, arrived):
        if arrived:
            kept = (pick(self.first, self.where[self.axes[0]]), pick(self.second, self.where[self.axes[1]]))
            self.sums = tuple(k.astype(F32) + m.astype(F32) for k, m in zip(kept, arrived))
        self.first, self.second = (part.astype(BF) for part in self.sums)
        self.axes = self.axes[::-1]

    def finish(self):
        both = jnp.concatenate([self.first, self.second], axis=1)
        return scatter_axis(both, 3, self.sizes, self.where)


def tied(first, second):
    return lax.optimization_barrier((first, second))


def halo_tokens(tokens, reach):
    pieces = [tokens]
    for _ in range(reach):
        pieces.insert(0, passed_along(pieces[0], "group", 1))
    return jnp.concatenate(pieces, axis=0)


def halo_return(rows, own):
    reach = rows.shape[0] // own - 1
    carried = None
    for slot in range(reach):
        piece = rows[slot * own : (slot + 1) * own]
        if carried is not None:
            piece = (piece.astype(F32) + carried.astype(F32)).astype(BF)
        carried = passed_along(piece, "group", -1)
    total = rows[reach * own :].astype(F32)
    return total if carried is None else total + carried.astype(F32)


def shards(tokens, cotangent, positions, attn_weights, ffn_weights, attn_m, attn_v, ffn_m, ffn_v):
    sizes, where = grid_of()
    core = where[2].astype(jnp.int32).reshape(1)
    attn_own, ffn_own = (attn_weights.shape[0], ffn_weights.shape[0])
    devices = math.prod(sizes)
    own = tokens.shape[0]
    reach = (WINDOW - 1) // own + 1

    ffn_full = lax.all_gather(ffn_weights.astype(BF), ("dp", "group"), axis=0)
    window = halo_tokens(tokens, reach)
    place = positions[:, None]
    before = positions[0] + jnp.arange(-reach * own, 0, dtype=positions.dtype)
    cosine, sine_t = rope_tables(jnp.concatenate([before, positions]))

    block = jnp.pad(attn_weights.astype(BF), ((0, rows_up(attn_own) - attn_own), (0, 0)))
    dims = attn_shapes()[:4]
    parts = unpack(
        functools.partial(unpack_pieces_body, dims, attn_own, sizes),
        dims,
        14,
        attn_own,
        devices,
        gather_pieces(block, sizes),
        (jnp.stack(where[:3]).astype(jnp.int32),),
    )
    attn_parts = parts[:4] + cut_gains(parts[4], (D, HD, HD, D))
    normed_b, queries, keys, query_b, key_b, value_b, attended_b, branch, middle = attention(
        window, place, cosine, sine_t, attn_parts
    )

    ffn_full, middle = tied(ffn_full, middle)
    dims = ffn_shapes()[:3]
    parts = unpack(
        functools.partial(unpack_whole_body, dims, ffn_own), dims, 10, ffn_own, devices, [ffn_full]
    )
    ffn_parts = parts[:3] + cut_gains(parts[3], (D, D))
    (
        output, pre_b, hidden_b, grad_ffn_b, grad_gate_b, grad_upper_b, grad_middle, sum_pre, sum_post,
    ) = feed_forward(middle, cotangent, ffn_parts)
    pair = pack_grads(
        ffn_shapes()[:3],
        [pre_b, pre_b, hidden_b],
        [grad_gate_b, grad_upper_b, grad_ffn_b],
        jnp.concatenate([sum_pre, sum_post], axis=1).reshape(-1, 128),
        ffn_own,
        sizes,
        core,
    )
    ffn_sum = Summing(pair, sizes, where)
    loads, grad_middle = tied(ffn_sum.load(), grad_middle)
    moved = ffn_sum.move(loads)
    kept = (queries, keys, query_b, key_b, value_b)
    (
        grad_branch_b, grad_q_b, grad_k_b, grad_v_b, grad_normed, sum_in, sum_q, sum_k, sum_mid,
    ) = attention_back(grad_middle, branch, window, place, cosine, sine_t, kept, attn_parts)
    pair = pack_grads(
        attn_shapes()[:4],
        [normed_b[reach * own :], normed_b, normed_b, attended_b],
        [grad_q_b, grad_k_b, grad_v_b, grad_branch_b],
        jnp.concatenate([sum_in, sum_q, sum_k, sum_mid], axis=1).reshape(-1, 128),
        attn_own,
        sizes,
        core,
    )
    moved, pair = tied(moved, pair)
    ffn_sum.add(moved)
    ffn_sum.add(ffn_sum.move(ffn_sum.load()))
    attn_sum = Summing(pair, sizes, where)
    for _ in range(2):
        attn_sum.add(attn_sum.move(attn_sum.load()))
    ffn_grad = ffn_sum.finish()[:ffn_own]
    attn_grad = attn_sum.finish()[:attn_own]

    grad_kv = halo_return(jnp.concatenate([grad_k_b, grad_v_b], axis=1), own).astype(BF)
    w_k, w_v, g_in = attn_parts[1], attn_parts[2], attn_parts[4]
    grad_normed = (
        grad_normed + times_trans(grad_kv[:, :HD], w_k) + times_trans(grad_kv[:, HD:], w_v)
    )
    values = tokens.astype(F32)
    grad_tokens = grad_middle + norm_grad(values, row_norm(values), g_in, grad_normed)[0]
    attn_new, attn_m_new, attn_v_new = adam_step(attn_weights, attn_grad, attn_m, attn_v)
    ffn_new, ffn_m_new, ffn_v_new = adam_step(ffn_weights, ffn_grad, ffn_m, ffn_v)
    return (
        output,
        grad_tokens,
        attn_grad,
        ffn_grad,
        attn_new,
        ffn_new,
        attn_m_new,
        attn_v_new,
        ffn_m_new,
        ffn_v_new,
    )


def solution(mesh):
    placed = (
        P(("dp", "group"), None),
        P(("dp", "group"), None),
        P(("dp", "group")),
        P(("dp", "group"), None),
        P(("dp", "group"), None),
        P(("dp", "group"), None),
        P(("dp", "group"), None),
        P(("dp", "group"), None),
        P(("dp", "group"), None),
    )
    return jax.shard_map(
        shards,
        mesh=mesh,
        in_specs=placed,
        out_specs=(
            P(("dp", "group"), None),
            P(("dp", "group"), None),
            P(("dp", "group"), None),
            P(("dp", "group"), None),
            P(("dp", "group"), None),
            P(("dp", "group"), None),
            P(("dp", "group"), None),
            P(("dp", "group"), None),
            P(("dp", "group"), None),
            P(("dp", "group"), None),
        ),
        check_vma=False,
    )
```

```python
import functools
import math

import jax
import jax.numpy as jnp
from jax import lax
from jax.experimental import pallas as pl
from jax.experimental.pallas import tpu as pltpu
from jax.sharding import PartitionSpec as P

D = 640
H = 4
HD = 256
FF = 2048
WINDOW = 512
STEP = 3


NORM_EPS = 1e-06
THETA = 10000.0
BETA_ONE = 0.9
BETA_TWO = 0.95
LEARN_RATE = 0.02
WEIGHT_DECAY = 0.1
ADAM_EPS = 1e-08
GELU_COEF = 0.7978845608028654


def passed_along(shard, axis, by):
    count = lax.axis_size(axis)
    pairs = [(i, i + by) for i in range(count) if 0 <= i + by < count]
    return lax.ppermute(shard, axis, pairs)


def attn_shapes():
    return [(D, H * HD), (D, HD), (D, HD), (H * HD, D), (D,), (HD,), (HD,), (D,)]


def ffn_shapes():
    return [(D, FF), (D, FF), (FF, D), (D,), (D,)]


def rope_tables(positions):
    half_dim = HD // 2
    freqs = jnp.power(THETA, -2.0 * jnp.arange(half_dim, dtype=jnp.float32) / HD)
    angles = positions.astype(jnp.float32)[:, None] * freqs[None, :]
    return (jnp.cos(angles), jnp.sin(angles))


def gelu_pair(values):
    tangent = jnp.tanh(GELU_COEF * (values + 0.044715 * (values * values * values)))
    activated = 0.5 * values * (1.0 + tangent)
    slope_v = 0.5 * (1.0 + tangent) + 0.5 * values * (1.0 - tangent * tangent) * GELU_COEF * (
        1.0 + 3.0 * 0.044715 * values * values
    )
    return (activated, slope_v)


def times_trans(left, right):
    return lax.dot_general(
        left, right, (((1,), (1,)), ((), ())), preferred_element_type=jnp.float32
    )


def adam_step(param, grad_in, moment_one, moment_two):
    new_one = BETA_ONE * moment_one + (1.0 - BETA_ONE) * grad_in
    new_two = BETA_TWO * moment_two + (1.0 - BETA_TWO) * grad_in * grad_in
    corr_one = new_one / (1.0 - BETA_ONE**STEP)
    corr_two = new_two / (1.0 - BETA_TWO**STEP)
    new_param = param - LEARN_RATE * (
        corr_one / (jnp.sqrt(corr_two) + ADAM_EPS) + WEIGHT_DECAY * param
    )
    return (new_param, new_one, new_two)


BF = jnp.bfloat16
F32 = jnp.float32
VMEM_LIMIT = 60 * 1024 * 1024


def rows_up(count, unit=16):
    return -(-count // unit) * unit


def pack_body(jobs, own, padded, sizes, core_ref, *refs):
    count = len(jobs)
    lefts, rights, gains = refs[:count], refs[count : 2 * count], refs[2 * count]
    send_ref, keep_ref, flat = refs[2 * count + 1 :]
    offset = 0
    tile = 128
    for (m, n), left, right in zip(jobs, lefts, rights):
        per_row = n // 128

        def step(i, carry, left=left, right=right, per_row=per_row, offset=offset):
            start = pl.multiple_of(i * tile, tile)
            block = lax.dot_general(
                left[:, pl.ds(start, tile)],
                right[...],
                (((0,), (0,)), ((), ())),
                preferred_element_type=F32,
            )
            base = offset + i * (tile * per_row)
            for j in range(per_row):
                flat[pl.ds(base + j, tile, stride=per_row), :] = block[:, 128 * j : 128 * j + 128]
            return carry

        lax.fori_loop(0, m // tile, step, 0)
        offset = offset + m * per_row
    tail = flat.shape[0] - offset
    flat[pl.ds(offset, tail), :] = jnp.zeros((tail, 128), F32)
    flat[pl.ds(offset, gains.shape[0]), :] = gains[...]
    slow, fast, cores, depth = sizes
    half = slow * fast * depth
    core = core_ref[0]

    def cut(i, carry):
        lead, z = i // depth, i % depth
        mine = ((lead * 2 + core) * depth + z) * own
        other = ((lead * 2 + 1 - core) * depth + z) * own
        keep_ref[i] = flat[pl.ds(mine, padded), :].astype(BF)
        send_ref[i] = flat[pl.ds(other, padded), :].astype(BF)
        return carry

    lax.fori_loop(0, half, cut, 0)


def pack_grads(jobs, lefts, rights, gains, own, sizes, core):
    padded = rows_up(own)
    devices = math.prod(sizes)
    half = devices // 2
    whole = rows_up(devices * own + 16, 8)
    out = jax.ShapeDtypeStruct((half, padded, 128), BF)
    vmem = pl.BlockSpec(memory_space=pltpu.VMEM)
    flops = sum(2 * m * n * lefts[0].shape[0] for m, n in jobs)
    return pl.pallas_call(
        functools.partial(pack_body, jobs, own, padded, sizes),
        out_shape=(out, out),
        in_specs=[pl.BlockSpec(memory_space=pltpu.SMEM)] + [vmem] * (2 * len(jobs) + 1),
        out_specs=(vmem, vmem),
        scratch_shapes=[pltpu.VMEM((whole, 128), F32)],
        compiler_params=pltpu.CompilerParams(vmem_limit_bytes=VMEM_LIMIT),
        cost_estimate=pl.CostEstimate(
            flops=flops, bytes_accessed=devices * padded * 256, transcendentals=0
        ),
    )(core, *lefts, *rights, gains)


def spread(flat, dims_list, outs):
    offset = 0
    tile = 128
    for (m, n), out in zip(dims_list, outs):
        per_row = n // 128

        def step(i, carry, out=out, per_row=per_row, offset=offset):
            start = pl.multiple_of(i * tile, tile)
            base = offset + i * (tile * per_row)
            for j in range(per_row):
                piece = flat[pl.ds(base + j, tile, stride=per_row), :]
                out[pl.ds(start, tile), 128 * j : 128 * j + 128] = piece.astype(BF)
            return carry

        lax.fori_loop(0, m // tile, step, 0)
        offset = offset + m * per_row
    outs[-1][...] = flat[pl.ds(offset, outs[-1].shape[0]), :]


def unpack_whole_body(dims_list, own, blocks, *refs):
    outs, flat = refs[:-1], refs[-1]

    def put(d, carry):
        flat[pl.ds(d * own, own), :] = blocks[d].astype(F32)
        return carry

    lax.fori_loop(0, blocks.shape[0], put, 0)
    spread(flat, dims_list, outs)


def unpack_pieces_body(dims_list, own, sizes, at_ref, *refs):
    first, first_far, second, second_far = refs[:4]
    outs, flat = refs[4:-1], refs[-1]
    slow, fast, cores, depth = sizes
    head = first.shape[1]
    near = tuple(at_ref[i] for i in range(3))

    def seen(extent, owner, here):
        return owner ^ here if extent == 2 else owner

    def put(i, carry):
        z, b, a = i % depth, (i // depth) % fast, i // (depth * fast)
        ra, rb = seen(slow, a, near[0]), seen(fast, b, near[1])
        one = (ra * fast + rb) * depth + z
        two = (rb * slow + ra) * depth + z
        for core, left, right in ((near[2], first, second), (1 - near[2], first_far, second_far)):
            base = (((a * fast + b) * 2 + core) * depth + z) * own
            flat[pl.ds(base, head), :] = left[one].astype(F32)
            flat[pl.ds(base + head, own - head), :] = right[two, : own - head].astype(F32)
        return carry

    lax.fori_loop(0, slow * fast * depth, put, 0)
    spread(flat, dims_list, outs)


def unpack(body, dims_list, gain_rows, own, devices, ins, scalars=()):
    vmem = pl.BlockSpec(memory_space=pltpu.VMEM)
    outs = [jax.ShapeDtypeStruct(dims, BF) for dims in dims_list]
    outs.append(jax.ShapeDtypeStruct((rows_up(gain_rows, 8), 128), F32))
    return pl.pallas_call(
        body,
        out_shape=tuple(outs),
        in_specs=[pl.BlockSpec(memory_space=pltpu.SMEM)] * len(scalars) + [vmem] * len(ins),
        out_specs=tuple([vmem] * len(outs)),
        scratch_shapes=[pltpu.VMEM((rows_up(devices * own + 8, 8), 128), F32)],
        compiler_params=pltpu.CompilerParams(vmem_limit_bytes=VMEM_LIMIT),
        cost_estimate=pl.CostEstimate(
            flops=0, bytes_accessed=devices * own * 512, transcendentals=0
        ),
    )(*scalars, *ins)


def contract(left, right, left_dim, right_dim):
    return lax.dot_general(
        left, right, (((left_dim,), (right_dim,)), ((), ())), preferred_element_type=F32
    )


def row_norm(values):
    return lax.rsqrt(jnp.mean(values * values, axis=-1, keepdims=True) + NORM_EPS)


def turn(values, cosine, sine_t, sign):
    first, second = values[:, : HD // 2], values[:, HD // 2 :]
    return jnp.concatenate(
        [first * cosine - sign * (second * sine_t), second * cosine + sign * (first * sine_t)],
        axis=-1,
    )


def seen_keys(reach, place, own, window):
    gap = lax.broadcasted_iota(jnp.int32, (own, window), 0) + (window - own)
    gap = gap - lax.broadcasted_iota(jnp.int32, (own, window), 1)
    return (gap >= 0) & (gap <= jnp.minimum(place, reach - 1))


def norm_grad(values, recip, gain, grad_out):
    scaled = grad_out * (1.0 + gain)
    grad_in = recip * scaled - values * recip * recip * recip * jnp.mean(
        scaled * values, axis=-1, keepdims=True
    )
    return grad_in, jnp.sum(grad_out * values * recip, axis=0, keepdims=True)


def attention_body(
    tokens, place, cosine, sine_t, w_q, w_k, w_v, w_o, g_in, g_q, g_k, g_mid,
    normed_b, queries, keys, query_b, key_b, value_b, attended_b, branch, middle,
):
    window, own = tokens.shape[0], place.shape[0]
    start = window - own
    values = tokens[...].astype(F32)
    normed_b[...] = (values * row_norm(values) * (1.0 + g_in[...])).astype(BF)
    keys[...] = contract(normed_b[...], w_k[...], 1, 0)
    value_b[...] = contract(normed_b[...], w_v[...], 1, 0).astype(BF)
    keyed = keys[...]
    keyed = keyed * row_norm(keyed) * (1.0 + g_k[...])
    key_b[...] = turn(keyed, cosine[...], sine_t[...], 1.0).astype(BF)
    queries[...] = contract(normed_b[start:, :], w_q[...], 1, 0)

    def head(h, carry):
        at = pl.ds(pl.multiple_of(h * HD, HD), HD)
        asked = queries[:, at]
        asked = asked * row_norm(asked) * (1.0 + g_q[...])
        asked = turn(asked, cosine[start:, :], sine_t[start:, :], 1.0) * (HD ** (-0.5))
        query_b[:, at] = asked.astype(BF)
        visible = seen_keys(WINDOW, place[...], own, window)
        scores = contract(query_b[:, at], key_b[...], 1, 1)
        total = jnp.sum(jnp.where(visible, jnp.exp(scores), 0.0), axis=-1, keepdims=True)
        prob = jnp.where(visible, jnp.exp(scores - jnp.log(total)), 0.0)
        attended_b[:, at] = contract(prob.astype(BF), value_b[...], 1, 0).astype(BF)
        return carry

    lax.fori_loop(0, H, head, 0)
    branch[...] = contract(attended_b[...], w_o[...], 1, 0)
    out = branch[...]
    middle[...] = values[start:, :] + out * row_norm(out) * (1.0 + g_mid[...])


def attention_back_body(
    grad_middle, branch, tokens, place, cosine, sine_t, queries, keys, query_b, key_b, value_b,
    w_q, w_k, w_v, w_o, g_in, g_q, g_k, g_mid,
    grad_branch_b, grad_q_b, grad_k_b, grad_v_b, grad_normed, sum_in, sum_q, sum_k, sum_mid,
    grad_key, grad_value,
):
    window, own = tokens.shape[0], place.shape[0]
    start = window - own
    out = branch[...]
    grad_branch, sum_mid[...] = norm_grad(out, row_norm(out), g_mid[...], grad_middle[...])
    grad_branch_b[...] = grad_branch.astype(BF)
    grad_key[...] = jnp.zeros_like(grad_key)
    grad_value[...] = jnp.zeros_like(grad_value)
    sum_q[...] = jnp.zeros_like(sum_q)

    def head(h, carry):
        at = pl.ds(pl.multiple_of(h * HD, HD), HD)
        grad_att = contract(grad_branch_b[...], w_o[at, :], 1, 1).astype(BF)
        visible = seen_keys(WINDOW, place[...], own, window)
        scores = contract(query_b[:, at], key_b[...], 1, 1)
        total = jnp.sum(jnp.where(visible, jnp.exp(scores), 0.0), axis=-1, keepdims=True)
        prob = jnp.where(visible, jnp.exp(scores - jnp.log(total)), 0.0)
        grad_prob = contract(grad_att, value_b[...], 1, 1)
        row_dot = jnp.sum(prob * grad_prob, axis=-1, keepdims=True)
        grad_score = (prob * (grad_prob - row_dot)).astype(BF)
        grad_query = contract(grad_score, key_b[...], 1, 0)
        grad_key[...] += contract(grad_score, query_b[:, at], 0, 0)
        grad_value[...] += contract(prob.astype(BF), grad_att, 0, 0)
        back = turn(grad_query * (HD ** (-0.5)), cosine[start:, :], sine_t[start:, :], -1.0)
        asked = queries[:, at]
        grad_q, part = norm_grad(asked, row_norm(asked), g_q[...], back)
        grad_q_b[:, at] = grad_q.astype(BF)
        sum_q[...] += part
        return carry

    lax.fori_loop(0, H, head, 0)
    keyed = keys[...]
    back = turn(grad_key[...], cosine[...], sine_t[...], -1.0)
    grad_k, sum_k[...] = norm_grad(keyed, row_norm(keyed), g_k[...], back)
    grad_k_b[...] = grad_k.astype(BF)
    grad_v_b[...] = grad_value[...].astype(BF)
    grad_normed[...] = contract(grad_q_b[...], w_q[...], 1, 1)
    through = contract(grad_k_b[...], w_k[...], 1, 1) + contract(grad_v_b[...], w_v[...], 1, 1)
    values = tokens[...].astype(F32)
    scaled = values * row_norm(values)
    sum_in[...] = jnp.sum(through * scaled, axis=0, keepdims=True) + jnp.sum(
        grad_normed[...] * scaled[start:, :], axis=0, keepdims=True
    )


def in_vmem(body, outs, scratch, flops, args):
    vmem = pl.BlockSpec(memory_space=pltpu.VMEM)
    out_shape = tuple(jax.ShapeDtypeStruct(shape, kind) for shape, kind in outs)
    moved = sum(math.prod(o.shape) * o.dtype.itemsize for o in (*out_shape, *args))
    return pl.pallas_call(
        body,
        out_shape=out_shape,
        in_specs=[vmem] * len(args),
        out_specs=tuple([vmem] * len(outs)),
        scratch_shapes=[pltpu.VMEM(shape, F32) for shape in scratch],
        compiler_params=pltpu.CompilerParams(vmem_limit_bytes=VMEM_LIMIT),
        cost_estimate=pl.CostEstimate(flops=flops, bytes_accessed=moved, transcendentals=0),
    )(*args)


def attention(tokens, place, cosine, sine_t, weights):
    window, own = tokens.shape[0], place.shape[0]
    outs = [
        ((window, D), BF), ((own, H * HD), F32), ((window, HD), F32), ((own, H * HD), BF),
        ((window, HD), BF), ((window, HD), BF), ((own, H * HD), BF), ((own, D), F32), ((own, D), F32),
    ]
    flops = 4 * own * window * H * HD + 4 * own * D * H * HD + 4 * window * D * HD
    return in_vmem(attention_body, outs, (), flops, (tokens, place, cosine, sine_t, *weights))


def attention_back(grad_middle, branch, tokens, place, cosine, sine_t, kept, weights):
    window, own = tokens.shape[0], place.shape[0]
    outs = [
        ((own, D), BF), ((own, H * HD), BF), ((window, HD), BF), ((window, HD), BF), ((own, D), F32),
        ((1, D), F32), ((1, HD), F32), ((1, HD), F32), ((1, D), F32),
    ]
    flops = 10 * own * window * H * HD + 4 * own * D * H * HD + 4 * window * D * HD
    args = (grad_middle, branch, tokens, place, cosine, sine_t, *kept, *weights)
    return in_vmem(attention_back_body, outs, ((window, HD), (window, HD)), flops, args)


def feed_forward_body(
    middle, top_in, w_g, w_u, w_d, g_pre, g_post,
    output, pre_b, hidden_b, grad_ffn_b, grad_gate_b, grad_upper_b, grad_middle, sum_pre, sum_post,
    gate, upper, total,
):
    tile = 512
    steps = gate.shape[1] // tile
    values = middle[...]
    recip = row_norm(values)
    pre_b[...] = (values * recip * (1.0 + g_pre[...])).astype(BF)
    total[...] = jnp.zeros_like(total)

    def forward(t, carry):
        at = pl.ds(pl.multiple_of(t * tile, tile), tile)
        gate_t = contract(pre_b[...], w_g[:, at], 1, 0)
        upper_t = contract(pre_b[...], w_u[:, at], 1, 0)
        gate[:, at] = gate_t
        upper[:, at] = upper_t
        activated, _ = gelu_pair(gate_t)
        hidden_b[:, at] = (activated * upper_t).astype(BF)
        total[...] += contract(hidden_b[:, at], w_d[at, :], 1, 0)
        return carry

    lax.fori_loop(0, steps, forward, 0)
    ffn_out = total[...]
    recip_post = row_norm(ffn_out)
    output[...] = (values + ffn_out * recip_post * (1.0 + g_post[...])).astype(BF)
    top = top_in[...].astype(F32)
    grad_ffn, sum_post[...] = norm_grad(ffn_out, recip_post, g_post[...], top)
    grad_ffn_b[...] = grad_ffn.astype(BF)
    total[...] = jnp.zeros_like(total)

    def backward(t, carry):
        at = pl.ds(pl.multiple_of(t * tile, tile), tile)
        grad_hidden = contract(grad_ffn_b[...], w_d[at, :], 1, 1)
        activated, slope = gelu_pair(gate[:, at])
        grad_gate_b[:, at] = (grad_hidden * upper[:, at] * slope).astype(BF)
        grad_upper_b[:, at] = (grad_hidden * activated).astype(BF)
        total[...] += contract(grad_gate_b[:, at], w_g[:, at], 1, 1)
        total[...] += contract(grad_upper_b[:, at], w_u[:, at], 1, 1)
        return carry

    lax.fori_loop(0, steps, backward, 0)
    grad_add, sum_pre[...] = norm_grad(values, recip, g_pre[...], total[...])
    grad_middle[...] = top + grad_add


def feed_forward(middle, cotangent, weights):
    own = middle.shape[0]
    outs = [
        ((own, D), BF), ((own, D), BF), ((own, FF), BF), ((own, D), BF), ((own, FF), BF),
        ((own, FF), BF), ((own, D), F32), ((1, D), F32), ((1, D), F32),
    ]
    scratch = ((own, FF), (own, FF), (own, D))
    return in_vmem(
        feed_forward_body, outs, scratch, 12 * own * D * FF, (middle, cotangent, *weights)
    )


def cut_gains(rows, lengths):
    line = rows.reshape(-1)
    starts = [sum(lengths[:i]) for i in range(len(lengths))]
    return tuple(line[a : a + b].reshape(1, b) for a, b in zip(starts, lengths))


def grid_of():
    pairs = lax.axis_size("dp") // 2
    slow = math.isqrt(pairs)
    fast = pairs // slow
    depth = lax.axis_size("group")
    place = lax.axis_index("dp")
    where = (place // (2 * fast), (place // 2) % fast, place % 2, lax.axis_index("group"))
    return ((slow, fast, 2, depth), where)


def step_along(value, axis, by, sizes, senders=None):
    extent = sizes[axis]
    pairs = []
    if axis == 3:
        for i in range(extent):
            if 0 <= i + by < extent and (senders is None or i in senders):
                pairs.append((i, i + by))
        return lax.ppermute(value, "group", pairs)
    stride = (2 * sizes[1], 2, 1)[axis]
    for i in range(sizes[0] * sizes[1] * 2):
        at = (i // stride) % extent
        if 0 <= at + by < extent and (senders is None or at in senders):
            pairs.append((i, i + by * stride))
    return lax.ppermute(value, "dp", pairs)


def swap_along(value, axis, sizes):
    stride = (2 * sizes[1], 2, 1)[axis]
    count = sizes[0] * sizes[1] * 2
    pairs = [(i, i + stride * (1 - 2 * ((i // stride) % 2))) for i in range(count)]
    return lax.ppermute(value, "dp", pairs)


def gather_axis(value, axis, sizes):
    extent = sizes[axis]
    if extent == 2:
        return jnp.stack([value, swap_along(value, axis, sizes)])
    stride = (2 * sizes[1], 2, 1)[axis]
    count = sizes[0] * sizes[1] * 2
    groups = [
        [i + k * stride for k in range(extent)] for i in range(count) if (i // stride) % extent == 0
    ]
    return lax.all_gather(value, "dp", axis=0, axis_index_groups=groups)


def gather_pieces(line, sizes):
    head = line.shape[1] // 32 * 16
    pieces = []
    for part, order in ((line[:, :head], (1, 0)), (line[:, head:], (0, 1))):
        for axis in order:
            part = gather_axis(part, axis, sizes)
        part = part.reshape(-1, *part.shape[-2:])
        pieces += [part, swap_along(part, 2, sizes)]
    return pieces


def swap_line(value, bit, sizes):
    return lax.ppermute(value, "group", [(i, i ^ bit) for i in range(sizes[3])])


def pick(blocks, index, axis=0):
    return lax.dynamic_index_in_dim(blocks, index, axis=axis, keepdims=False)


def scatter_axis(blocks, axis, sizes, where):
    extent, at = (sizes[axis], where[axis])
    if extent == 1:
        return blocks[0].astype(jnp.float32)
    if extent == 2 and axis < 3:
        arrived = swap_along(pick(blocks, 1 - at), axis, sizes)
        return pick(blocks, at).astype(jnp.float32) + arrived.astype(jnp.float32)
    total = pick(blocks, at).astype(jnp.float32)
    for by in (1, -1):
        arrived = None
        for step in range(1, extent):
            dest = jnp.clip(at + by * (extent - step), 0, extent - 1)
            load = pick(blocks, dest)
            if arrived is not None:
                load = (load.astype(jnp.float32) + arrived.astype(jnp.float32)).astype(jnp.bfloat16)
            senders = range(step) if by == 1 else range(extent - step, extent)
            arrived = step_along(load, axis, by, sizes, senders)
        total = total + arrived.astype(jnp.float32)
    return total


class Summing:
    def __init__(self, pair, sizes, where):
        self.send, self.keep = pair
        self.sizes, self.where, self.stage = sizes, where, 0

    def axes(self):
        return (0, 1) if self.stage == 1 else (1, 0)

    def loads(self):
        if self.stage == 0:
            return (self.send,)
        if self.stage <= 2:
            if self.sizes[0] != 2 or self.sizes[1] != 2:
                return ()
            near, far = self.axes()
            return (pick(self.first, 1 - self.where[near]), pick(self.second, 1 - self.where[far]))
        return (self.side(1),)

    def side(self, other):
        index = lax.rem(self.where[3] // 2 ** (self.stage - 3) + other, 2)
        return pick(self.both.reshape(-1, 2, *self.both.shape[1:]), index, axis=1)

    def move(self, loads):
        if self.stage == 0:
            return (swap_along(loads[0], 2, self.sizes),)
        if self.stage <= 2:
            return tuple(swap_along(load, axis, self.sizes) for load, axis in zip(loads, self.axes()))
        return (swap_line(loads[0], 2 ** (self.stage - 3), self.sizes),)

    def add(self, arrived):
        if self.stage == 0:
            total = (self.keep.astype(F32) + arrived[0].astype(F32)).astype(BF)
            held = total.reshape(self.sizes[0], self.sizes[1], self.sizes[3], *total.shape[1:])
            cut = held.shape[3] // 32 * 16
            self.first = held[:, :, :, :cut]
            self.second = held[:, :, :, cut:].transpose(1, 0, 2, 3, 4)
        elif self.stage <= 2:
            parts = []
            for i, (part, axis) in enumerate(zip((self.first, self.second), self.axes())):
                if arrived:
                    part = pick(part, self.where[axis]).astype(F32) + arrived[i].astype(F32)
                else:
                    part = scatter_axis(part, axis, self.sizes, self.where)
                parts.append(part.astype(BF))
            self.first, self.second = parts
            if self.stage == 2:
                self.both = jnp.concatenate(parts, axis=1)
        else:
            total = self.side(0).astype(F32) + arrived[0].astype(F32)
            self.both = total.astype(BF)
            self.total = total
        self.stage += 1

    def result(self):
        return (self.total if self.sizes[3] > 1 else self.both.astype(F32))[0]


def after(value, other):
    return lax.optimization_barrier((value, other))[0]


def advance(*sums):
    loads = lax.optimization_barrier(tuple(one.loads() for one in sums))
    moved = tuple(one.move(load) for one, load in zip(sums, loads))
    for one, came in zip(sums, lax.optimization_barrier(moved)):
        one.add(came)


def tied(first, second):
    return lax.optimization_barrier((first, second))


def halo_tokens(tokens, reach):
    pieces = [tokens]
    for _ in range(reach):
        pieces.insert(0, passed_along(pieces[0], "group", 1))
    return jnp.concatenate(pieces, axis=0)


def halo_return(rows, own):
    reach = rows.shape[0] // own - 1
    carried = None
    for slot in range(reach):
        piece = rows[slot * own : (slot + 1) * own]
        if carried is not None:
            piece = (piece.astype(F32) + carried.astype(F32)).astype(BF)
        carried = passed_along(piece, "group", -1)
    total = rows[reach * own :].astype(F32)
    return total if carried is None else total + carried.astype(F32)


def shards(tokens, cotangent, positions, attn_weights, ffn_weights, attn_m, attn_v, ffn_m, ffn_v):
    sizes, where = grid_of()
    core = where[2].astype(jnp.int32).reshape(1)
    attn_own, ffn_own = (attn_weights.shape[0], ffn_weights.shape[0])
    devices = math.prod(sizes)
    own = tokens.shape[0]
    reach = (WINDOW - 1) // own + 1

    ffn_full = lax.all_gather(ffn_weights.astype(BF), ("dp", "group"), axis=0)
    window = halo_tokens(tokens, reach)
    place = positions[:, None]
    before = positions[0] + jnp.arange(-reach * own, 0, dtype=positions.dtype)
    cosine, sine_t = rope_tables(jnp.concatenate([before, positions]))

    block = jnp.pad(attn_weights.astype(BF), ((0, rows_up(attn_own) - attn_own), (0, 0)))
    line = lax.all_gather(block, "group", axis=0)
    here = jnp.stack(where).astype(jnp.int32)
    dims = attn_shapes()[:4]
    parts = unpack(
        functools.partial(unpack_pieces_body, dims, attn_own, sizes),
        dims,
        14,
        attn_own,
        devices,
        gather_pieces(line, sizes),
        (here,),
    )
    attn_parts = parts[:4] + cut_gains(parts[4], (D, HD, HD, D))
    normed_b, queries, keys, query_b, key_b, value_b, attended_b, branch, middle = attention(
        window, place, cosine, sine_t, attn_parts
    )

    ffn_full, middle = tied(ffn_full, middle)
    dims = ffn_shapes()[:3]
    parts = unpack(
        functools.partial(unpack_whole_body, dims, ffn_own), dims, 10, ffn_own, devices, [ffn_full]
    )
    ffn_parts = parts[:3] + cut_gains(parts[3], (D, D))
    (
        output, pre_b, hidden_b, grad_ffn_b, grad_gate_b, grad_upper_b, grad_middle, sum_pre, sum_post,
    ) = feed_forward(middle, cotangent, ffn_parts)
    pair = pack_grads(
        ffn_shapes()[:3],
        [pre_b, pre_b, hidden_b],
        [grad_gate_b, grad_upper_b, grad_ffn_b],
        jnp.concatenate([sum_pre, sum_post], axis=1).reshape(-1, 128),
        ffn_own,
        sizes,
        core,
    )
    ffn_sum = Summing(pair, sizes, where)
    advance(ffn_sum)
    loads, grad_middle = tied(ffn_sum.loads(), grad_middle)
    moved = ffn_sum.move(loads)
    kept = (queries, keys, query_b, key_b, value_b)
    (
        grad_branch_b, grad_q_b, grad_k_b, grad_v_b, grad_normed, sum_in, sum_q, sum_k, sum_mid,
    ) = attention_back(grad_middle, branch, window, place, cosine, sine_t, kept, attn_parts)
    moved, (grad_branch_b, grad_q_b) = tied(moved, (grad_branch_b, grad_q_b))
    ffn_sum.add(moved)
    loads, (grad_branch_b, grad_q_b) = tied(ffn_sum.loads(), (grad_branch_b, grad_q_b))
    moved = ffn_sum.move(loads)
    pair = pack_grads(
        attn_shapes()[:4],
        [normed_b[reach * own :], normed_b, normed_b, attended_b],
        [grad_q_b, grad_k_b, grad_v_b, grad_branch_b],
        jnp.concatenate([sum_in, sum_q, sum_k, sum_mid], axis=1).reshape(-1, 128),
        attn_own,
        sizes,
        core,
    )
    moved, pair = tied(moved, pair)
    ffn_sum.add(moved)
    attn_sum = Summing(pair, sizes, where)
    last = 3 + (sizes[3] - 1).bit_length()
    while attn_sum.stage < last:
        moved = ffn_sum.move(ffn_sum.loads()) if ffn_sum.stage < last else None
        if attn_sum.stage == 0:
            attn_sum.add(attn_sum.move(attn_sum.loads()))
        loads = attn_sum.loads()
        if moved is not None:
            ffn_sum.add(after(moved, loads))
        attn_sum.add(attn_sum.move(loads))
    while ffn_sum.stage < last:
        ffn_sum.add(ffn_sum.move(ffn_sum.loads()))
    ffn_grad = ffn_sum.result()[:ffn_own]
    attn_grad = attn_sum.result()[:attn_own]

    grad_kv = halo_return(jnp.concatenate([grad_k_b, grad_v_b], axis=1), own).astype(BF)
    w_k, w_v, g_in = attn_parts[1], attn_parts[2], attn_parts[4]
    grad_normed = (
        grad_normed + times_trans(grad_kv[:, :HD], w_k) + times_trans(grad_kv[:, HD:], w_v)
    )
    values = tokens.astype(F32)
    grad_tokens = grad_middle + norm_grad(values, row_norm(values), g_in, grad_normed)[0]
    attn_new, attn_m_new, attn_v_new = adam_step(attn_weights, attn_grad, attn_m, attn_v)
    ffn_new, ffn_m_new, ffn_v_new = adam_step(ffn_weights, ffn_grad, ffn_m, ffn_v)
    return (
        output,
        grad_tokens,
        attn_grad,
        ffn_grad,
        attn_new,
        ffn_new,
        attn_m_new,
        attn_v_new,
        ffn_m_new,
        ffn_v_new,
    )


def solution(mesh):
    placed = (
        P(("dp", "group"), None),
        P(("dp", "group"), None),
        P(("dp", "group")),
        P(("dp", "group"), None),
        P(("dp", "group"), None),
        P(("dp", "group"), None),
        P(("dp", "group"), None),
        P(("dp", "group"), None),
        P(("dp", "group"), None),
    )
    return jax.shard_map(
        shards,
        mesh=mesh,
        in_specs=placed,
        out_specs=(
            P(("dp", "group"), None),
            P(("dp", "group"), None),
            P(("dp", "group"), None),
            P(("dp", "group"), None),
            P(("dp", "group"), None),
            P(("dp", "group"), None),
            P(("dp", "group"), None),
            P(("dp", "group"), None),
            P(("dp", "group"), None),
            P(("dp", "group"), None),
        ),
        check_vma=False,
    )
```

```python
import functools
import math

import jax
import jax.numpy as jnp
from jax import lax
from jax.experimental import pallas as pl
from jax.experimental.pallas import tpu as pltpu
from jax.sharding import PartitionSpec as P


D = 640
H = 4
HD = 256
FF = 2048
WINDOW = 512
STEP = 3


NORM_EPS = 1e-06
THETA = 10000.0
BETA_ONE = 0.9
BETA_TWO = 0.95
LEARN_RATE = 0.02
WEIGHT_DECAY = 0.1
ADAM_EPS = 1e-08
GELU_COEF = 0.7978845608028654


def passed_along(shard, axis, by):
    count = lax.axis_size(axis)
    pairs = [(i, i + by) for i in range(count) if 0 <= i + by < count]
    return lax.ppermute(shard, axis, pairs)


def attn_shapes():
    return [(D, H * HD), (D, HD), (D, HD), (H * HD, D), (D,), (HD,), (HD,), (D,)]


def ffn_shapes():
    return [(D, FF), (D, FF), (FF, D), (D,), (D,)]


def rope_tables(positions):
    half_dim = HD // 2
    freqs = jnp.power(THETA, -2.0 * jnp.arange(half_dim, dtype=jnp.float32) / HD)
    angles = positions.astype(jnp.float32)[:, None] * freqs[None, :]
    return (jnp.cos(angles), jnp.sin(angles))


def gelu_pair(values):
    tangent = jnp.tanh(GELU_COEF * (values + 0.044715 * (values * values * values)))
    activated = 0.5 * values * (1.0 + tangent)
    slope_v = 0.5 * (1.0 + tangent) + 0.5 * values * (1.0 - tangent * tangent) * GELU_COEF * (
        1.0 + 3.0 * 0.044715 * values * values
    )
    return (activated, slope_v)


def times_trans(left, right):
    return lax.dot_general(
        left, right, (((1,), (1,)), ((), ())), preferred_element_type=jnp.float32
    )


def adam_step(param, grad_in, moment_one, moment_two):
    new_one = BETA_ONE * moment_one + (1.0 - BETA_ONE) * grad_in
    new_two = BETA_TWO * moment_two + (1.0 - BETA_TWO) * grad_in * grad_in
    corr_one = new_one / (1.0 - BETA_ONE**STEP)
    corr_two = new_two / (1.0 - BETA_TWO**STEP)
    new_param = param - LEARN_RATE * (
        corr_one / (jnp.sqrt(corr_two) + ADAM_EPS) + WEIGHT_DECAY * param
    )
    return (new_param, new_one, new_two)


BF = jnp.bfloat16
F32 = jnp.float32
VMEM_LIMIT = 60 * 1024 * 1024


def rows_up(count, unit=16):
    return -(-count // unit) * unit


def lay_out(jobs, lefts, rights, gains, flat):
    offset = 0
    tile = 128
    for (m, n), left, right in zip(jobs, lefts, rights):
        per_row = n // 128
        skip = left.shape[0] - right.shape[0]

        def step(i, carry, left=left, right=right, per_row=per_row, offset=offset, skip=skip):
            start = pl.multiple_of(i * tile, tile)
            block = contract(left[skip:, pl.ds(start, tile)], right[...], 0, 0)
            base = offset + i * (tile * per_row)
            for j in range(per_row):
                flat[pl.ds(base + j, tile, stride=per_row), :] = block[:, 128 * j : 128 * j + 128]
            return carry

        lax.fori_loop(0, m // tile, step, 0)
        offset = offset + m * per_row
    tail = flat.shape[0] - offset
    flat[pl.ds(offset, tail), :] = jnp.zeros((tail, 128), F32)
    for row in gains:
        for j in range(row.shape[1] // 128):
            flat[pl.ds(offset, 1), :] = row[:, 128 * j : 128 * j + 128]
            offset = offset + 1


def halves(padded):
    cut = padded // 32 * 16
    return (cut, padded - cut)


def cut_owners(flat, own, padded, sizes, core, outs):
    slow, fast, _, depth = sizes
    cut = halves(padded)[0]

    def step(i, carry):
        lead, z = i // depth, i % depth
        for which, (head, rest) in ((1 - core, outs[:2]), (core, outs[2:])):
            start = ((lead * 2 + which) * depth + z) * own
            block = flat[pl.ds(start, padded), :].astype(BF)
            head[i] = block[:cut]
            rest[i] = block[cut:]
        return carry

    lax.fori_loop(0, slow * fast * depth, step, 0)


def pack_body(jobs, own, padded, sizes, core_ref, *refs):
    count = len(jobs)
    lefts, rights, gains = refs[:count], refs[count : 2 * count], refs[2 * count : -5]
    outs, flat = refs[-5:-1], refs[-1]
    lay_out(jobs, lefts, rights, gains, flat)
    cut_owners(flat, own, padded, sizes, core_ref[0], outs)


def pack_grads(jobs, lefts, rights, gains, own, sizes, core):
    padded = rows_up(own)
    devices = math.prod(sizes)
    half = devices // 2
    whole = rows_up(devices * own + 16, 8)
    out = tuple(jax.ShapeDtypeStruct((half, rows, 128), BF) for rows in halves(padded)) * 2
    vmem = pl.BlockSpec(memory_space=pltpu.VMEM)
    flops = sum(2 * m * n * lefts[0].shape[0] for m, n in jobs)
    return pl.pallas_call(
        functools.partial(pack_body, jobs, own, padded, sizes),
        out_shape=out,
        in_specs=[pl.BlockSpec(memory_space=pltpu.SMEM)] + [vmem] * (2 * len(jobs) + len(gains)),
        out_specs=(vmem,) * 4,
        scratch_shapes=[pltpu.VMEM((whole, 128), F32)],
        compiler_params=pltpu.CompilerParams(vmem_limit_bytes=VMEM_LIMIT),
        cost_estimate=pl.CostEstimate(
            flops=flops, bytes_accessed=devices * padded * 256, transcendentals=0
        ),
    )(core, *lefts, *rights, *gains)


def spread(flat, dims_list, outs):
    offset = 0
    tile = 128
    for (m, n), out in zip(dims_list, outs):
        per_row = n // 128

        def step(i, carry, out=out, per_row=per_row, offset=offset):
            start = pl.multiple_of(i * tile, tile)
            base = offset + i * (tile * per_row)
            for j in range(per_row):
                piece = flat[pl.ds(base + j, tile, stride=per_row), :]
                out[pl.ds(start, tile), 128 * j : 128 * j + 128] = piece.astype(BF)
            return carry

        lax.fori_loop(0, m // tile, step, 0)
        offset = offset + m * per_row
    if len(outs) > len(dims_list):
        outs[-1][...] = flat[pl.ds(offset, outs[-1].shape[0]), :]
    return offset


def unpack_pieces_body(dims_list, own, sizes, at_ref, *refs):
    first, first_far, second, second_far = refs[:4]
    outs, flat = refs[4:-1], refs[-1]
    slow, fast, _, depth = sizes
    head = first.shape[1]
    near = tuple(at_ref[i] for i in range(3))

    def seen(extent, owner, here):
        return owner ^ here if extent == 2 else owner

    def put(i, carry):
        z, b, a = i % depth, (i // depth) % fast, i // (depth * fast)
        ra, rb = seen(slow, a, near[0]), seen(fast, b, near[1])
        one = (ra * fast + rb) * depth + z
        two = (rb * slow + ra) * depth + z
        for core, left, right in ((near[2], first, second), (1 - near[2], first_far, second_far)):
            base = (((a * fast + b) * 2 + core) * depth + z) * own
            flat[pl.ds(base, head), :] = left[one].astype(F32)
            flat[pl.ds(base + head, own - head), :] = right[two, : own - head].astype(F32)
        return carry

    lax.fori_loop(0, slow * fast * depth, put, 0)
    spread(flat, dims_list, outs)


def unpack(body, dims_list, gain_rows, own, devices, ins, scalars=()):
    vmem = pl.BlockSpec(memory_space=pltpu.VMEM)
    outs = [jax.ShapeDtypeStruct(dims, BF) for dims in dims_list]
    outs.append(jax.ShapeDtypeStruct((rows_up(gain_rows, 8), 128), F32))
    return pl.pallas_call(
        body,
        out_shape=tuple(outs),
        in_specs=[pl.BlockSpec(memory_space=pltpu.SMEM)] * len(scalars) + [vmem] * len(ins),
        out_specs=tuple([vmem] * len(outs)),
        scratch_shapes=[pltpu.VMEM((rows_up(devices * own + 8, 8), 128), F32)],
        compiler_params=pltpu.CompilerParams(vmem_limit_bytes=VMEM_LIMIT),
        cost_estimate=pl.CostEstimate(
            flops=0, bytes_accessed=devices * own * 512, transcendentals=0
        ),
    )(*scalars, *ins)


def contract(left, right, left_dim, right_dim):
    return lax.dot_general(
        left, right, (((left_dim,), (right_dim,)), ((), ())), preferred_element_type=F32
    )


def row_norm(values):
    return lax.rsqrt(jnp.mean(values * values, axis=-1, keepdims=True) + NORM_EPS)


def turn(values, cosine, sine_t, sign):
    first, second = values[:, : HD // 2], values[:, HD // 2 :]
    return jnp.concatenate(
        [first * cosine - sign * (second * sine_t), second * cosine + sign * (first * sine_t)],
        axis=-1,
    )


def seen_keys(reach, place, own, window):
    gap = lax.broadcasted_iota(jnp.int32, (own, window), 0) + (window - own)
    gap = gap - lax.broadcasted_iota(jnp.int32, (own, window), 1)
    return (gap >= 0) & (gap <= jnp.minimum(place, reach - 1))


def norm_grad(values, recip, gain, grad_out):
    scaled = grad_out * (1.0 + gain)
    grad_in = recip * scaled - values * recip * recip * recip * jnp.mean(
        scaled * values, axis=-1, keepdims=True
    )
    return grad_in, jnp.sum(grad_out * values * recip, axis=0, keepdims=True)


def attention_body(
    tokens, place, cosine, sine_t, w_q, w_k, w_v, w_o, g_in, g_q, g_k, g_mid,
    normed_b, queries, keys, query_b, key_b, value_b, attended_b, branch, middle,
):
    window, own = tokens.shape[0], place.shape[0]
    start = window - own
    values = tokens[...].astype(F32)
    normed_b[...] = (values * row_norm(values) * (1.0 + g_in[...])).astype(BF)
    keys[...] = contract(normed_b[...], w_k[...], 1, 0)
    value_b[...] = contract(normed_b[...], w_v[...], 1, 0).astype(BF)
    keyed = keys[...]
    keyed = keyed * row_norm(keyed) * (1.0 + g_k[...])
    key_b[...] = turn(keyed, cosine[...], sine_t[...], 1.0).astype(BF)
    queries[...] = contract(normed_b[start:, :], w_q[...], 1, 0)

    def head(h, carry):
        at = pl.ds(pl.multiple_of(h * HD, HD), HD)
        asked = queries[:, at]
        asked = asked * row_norm(asked) * (1.0 + g_q[...])
        asked = turn(asked, cosine[start:, :], sine_t[start:, :], 1.0) * (HD ** (-0.5))
        query_b[:, at] = asked.astype(BF)
        visible = seen_keys(WINDOW, place[...], own, window)
        scores = contract(query_b[:, at], key_b[...], 1, 1)
        total = jnp.sum(jnp.where(visible, jnp.exp(scores), 0.0), axis=-1, keepdims=True)
        prob = jnp.where(visible, jnp.exp(scores - jnp.log(total)), 0.0)
        attended_b[:, at] = contract(prob.astype(BF), value_b[...], 1, 0).astype(BF)
        return carry

    lax.fori_loop(0, H, head, 0)
    branch[...] = contract(attended_b[...], w_o[...], 1, 0)
    out = branch[...]
    middle[...] = values[start:, :] + out * row_norm(out) * (1.0 + g_mid[...])


def attention_back_body(
    grad_middle, branch, tokens, place, cosine, sine_t, queries, keys, query_b, key_b, value_b,
    w_q, w_k, w_v, w_o, g_in, g_q, g_k, g_mid,
    grad_branch_b, grad_q_b, grad_k_b, grad_v_b, grad_normed, sum_in, sum_q, sum_k, sum_mid,
    grad_key, grad_value,
):
    window, own = tokens.shape[0], place.shape[0]
    start = window - own
    out = branch[...]
    grad_branch, sum_mid[...] = norm_grad(out, row_norm(out), g_mid[...], grad_middle[...])
    grad_branch_b[...] = grad_branch.astype(BF)
    grad_key[...] = jnp.zeros_like(grad_key)
    grad_value[...] = jnp.zeros_like(grad_value)
    sum_q[...] = jnp.zeros_like(sum_q)

    def head(h, carry):
        at = pl.ds(pl.multiple_of(h * HD, HD), HD)
        grad_att = contract(grad_branch_b[...], w_o[at, :], 1, 1).astype(BF)
        visible = seen_keys(WINDOW, place[...], own, window)
        scores = contract(query_b[:, at], key_b[...], 1, 1)
        total = jnp.sum(jnp.where(visible, jnp.exp(scores), 0.0), axis=-1, keepdims=True)
        prob = jnp.where(visible, jnp.exp(scores - jnp.log(total)), 0.0)
        grad_prob = contract(grad_att, value_b[...], 1, 1)
        row_dot = jnp.sum(prob * grad_prob, axis=-1, keepdims=True)
        grad_score = (prob * (grad_prob - row_dot)).astype(BF)
        grad_query = contract(grad_score, key_b[...], 1, 0)
        grad_key[...] += contract(grad_score, query_b[:, at], 0, 0)
        grad_value[...] += contract(prob.astype(BF), grad_att, 0, 0)
        back = turn(grad_query * (HD ** (-0.5)), cosine[start:, :], sine_t[start:, :], -1.0)
        asked = queries[:, at]
        grad_q, part = norm_grad(asked, row_norm(asked), g_q[...], back)
        grad_q_b[:, at] = grad_q.astype(BF)
        sum_q[...] += part
        return carry

    lax.fori_loop(0, H, head, 0)
    keyed = keys[...]
    back = turn(grad_key[...], cosine[...], sine_t[...], -1.0)
    grad_k, sum_k[...] = norm_grad(keyed, row_norm(keyed), g_k[...], back)
    grad_k_b[...] = grad_k.astype(BF)
    grad_v_b[...] = grad_value[...].astype(BF)
    grad_normed[...] = contract(grad_q_b[...], w_q[...], 1, 1)
    through = contract(grad_k_b[...], w_k[...], 1, 1) + contract(grad_v_b[...], w_v[...], 1, 1)
    values = tokens[...].astype(F32)
    scaled = values * row_norm(values)
    sum_in[...] = jnp.sum(through * scaled, axis=0, keepdims=True) + jnp.sum(
        grad_normed[...] * scaled[start:, :], axis=0, keepdims=True
    )


def in_vmem(body, outs, scratch, flops, args):
    vmem = pl.BlockSpec(memory_space=pltpu.VMEM)
    out_shape = tuple(jax.ShapeDtypeStruct(shape, kind) for shape, kind in outs)
    moved = sum(math.prod(o.shape) * o.dtype.itemsize for o in (*out_shape, *args))
    return pl.pallas_call(
        body,
        out_shape=out_shape,
        in_specs=[vmem] * len(args),
        out_specs=tuple([vmem] * len(outs)),
        scratch_shapes=[pltpu.VMEM(shape, F32) for shape in scratch],
        compiler_params=pltpu.CompilerParams(vmem_limit_bytes=VMEM_LIMIT),
        cost_estimate=pl.CostEstimate(flops=flops, bytes_accessed=moved, transcendentals=0),
    )(*args)


def attention(tokens, place, cosine, sine_t, weights):
    window, own = tokens.shape[0], place.shape[0]
    outs = [
        ((window, D), BF), ((own, H * HD), F32), ((window, HD), F32), ((own, H * HD), BF),
        ((window, HD), BF), ((window, HD), BF), ((own, H * HD), BF), ((own, D), F32), ((own, D), F32),
    ]
    flops = 4 * own * window * H * HD + 4 * own * D * H * HD + 4 * window * D * HD
    return in_vmem(attention_body, outs, (), flops, (tokens, place, cosine, sine_t, *weights))


def attention_back(grad_middle, branch, tokens, place, cosine, sine_t, kept, weights):
    window, own = tokens.shape[0], place.shape[0]
    outs = [
        ((own, D), BF), ((own, H * HD), BF), ((window, HD), BF), ((window, HD), BF), ((own, D), F32),
        ((1, D), F32), ((1, HD), F32), ((1, HD), F32), ((1, D), F32),
    ]
    flops = 10 * own * window * H * HD + 4 * own * D * H * HD + 4 * window * D * HD
    args = (grad_middle, branch, tokens, place, cosine, sine_t, *kept, *weights)
    return in_vmem(attention_back_body, outs, ((window, HD), (window, HD)), flops, args)


def feed_forward_body(
    dims_list, own_rows, padded, sizes,
    core_ref, middle, top_in, blocks,
    output, grad_middle, send_head, send_rest, keep_head, keep_rest,
    flat, w_g, w_u, w_d, pre_b, hidden_b, grad_ffn_b, grad_gate_b, grad_upper_b, gate, upper, total,
):
    def put(d, carry):
        flat[pl.ds(d * own_rows, own_rows), :] = blocks[d].astype(F32)
        return carry

    lax.fori_loop(0, blocks.shape[0], put, 0)
    offset = spread(flat, dims_list, (w_g, w_u, w_d))
    rows = D // 128
    g_pre, g_post = (
        jnp.concatenate([flat[pl.ds(at + j, 1), :] for j in range(rows)], axis=1)
        for at in (offset, offset + rows)
    )
    tile = 512
    steps = gate.shape[1] // tile
    values = middle[...]
    recip = row_norm(values)
    pre_b[...] = (values * recip * (1.0 + g_pre)).astype(BF)
    total[...] = jnp.zeros_like(total)

    def forward(t, carry):
        at = pl.ds(pl.multiple_of(t * tile, tile), tile)
        gate_t = contract(pre_b[...], w_g[:, at], 1, 0)
        upper_t = contract(pre_b[...], w_u[:, at], 1, 0)
        gate[:, at] = gate_t
        upper[:, at] = upper_t
        activated, _ = gelu_pair(gate_t)
        hidden_b[:, at] = (activated * upper_t).astype(BF)
        total[...] += contract(hidden_b[:, at], w_d[at, :], 1, 0)
        return carry

    lax.fori_loop(0, steps, forward, 0)
    ffn_out = total[...]
    recip_post = row_norm(ffn_out)
    output[...] = (values + ffn_out * recip_post * (1.0 + g_post)).astype(BF)
    top = top_in[...].astype(F32)
    grad_ffn, sum_post = norm_grad(ffn_out, recip_post, g_post, top)
    grad_ffn_b[...] = grad_ffn.astype(BF)
    total[...] = jnp.zeros_like(total)

    def backward(t, carry):
        at = pl.ds(pl.multiple_of(t * tile, tile), tile)
        grad_hidden = contract(grad_ffn_b[...], w_d[at, :], 1, 1)
        activated, slope = gelu_pair(gate[:, at])
        grad_gate_b[:, at] = (grad_hidden * upper[:, at] * slope).astype(BF)
        grad_upper_b[:, at] = (grad_hidden * activated).astype(BF)
        total[...] += contract(grad_gate_b[:, at], w_g[:, at], 1, 1)
        total[...] += contract(grad_upper_b[:, at], w_u[:, at], 1, 1)
        return carry

    lax.fori_loop(0, steps, backward, 0)
    grad_add, sum_pre = norm_grad(values, recip, g_pre, total[...])
    grad_middle[...] = top + grad_add
    lay_out(
        dims_list,
        (pre_b, pre_b, hidden_b),
        (grad_gate_b, grad_upper_b, grad_ffn_b),
        (sum_pre, sum_post),
        flat,
    )
    outs = (send_head, send_rest, keep_head, keep_rest)
    cut_owners(flat, own_rows, padded, sizes, core_ref[0], outs)


def feed_forward(core, middle, cotangent, blocks, sizes):
    own = middle.shape[0]
    devices, own_rows = blocks.shape[:2]
    padded = rows_up(own_rows)
    dims_list = ffn_shapes()[:3]
    out = tuple(jax.ShapeDtypeStruct((devices // 2, rows, 128), BF) for rows in halves(padded)) * 2
    vmem = pl.BlockSpec(memory_space=pltpu.VMEM)
    scratch = [((rows_up(devices * own_rows + 16, 8), 128), F32)]
    scratch += [(dims, BF) for dims in dims_list]
    scratch += [((own, D), BF), ((own, FF), BF), ((own, D), BF), ((own, FF), BF), ((own, FF), BF)]
    scratch += [((own, FF), F32), ((own, FF), F32), ((own, D), F32)]
    return pl.pallas_call(
        functools.partial(feed_forward_body, dims_list, own_rows, padded, sizes),
        out_shape=(
            jax.ShapeDtypeStruct((own, D), BF), jax.ShapeDtypeStruct((own, D), F32), *out,
        ),
        in_specs=[pl.BlockSpec(memory_space=pltpu.SMEM)] + [vmem] * 3,
        out_specs=(vmem,) * 6,
        scratch_shapes=[pltpu.VMEM(shape, kind) for shape, kind in scratch],
        compiler_params=pltpu.CompilerParams(vmem_limit_bytes=VMEM_LIMIT),
        cost_estimate=pl.CostEstimate(
            flops=18 * own * D * FF, bytes_accessed=4 * blocks.size, transcendentals=own * FF
        ),
    )(core, middle, cotangent, blocks)


def cut_gains(rows, lengths):
    line = rows.reshape(-1)
    starts = [sum(lengths[:i]) for i in range(len(lengths))]
    return tuple(line[a : a + b].reshape(1, b) for a, b in zip(starts, lengths))


def grid_of():
    pairs = lax.axis_size("dp") // 2
    slow = math.isqrt(pairs)
    fast = pairs // slow
    depth = lax.axis_size("group")
    place = lax.axis_index("dp")
    where = (place // (2 * fast), (place // 2) % fast, place % 2, lax.axis_index("group"))
    return ((slow, fast, 2, depth), where)


def step_along(value, axis, by, sizes, senders=None):
    extent = sizes[axis]
    pairs = []
    if axis == 3:
        for i in range(extent):
            if 0 <= i + by < extent and (senders is None or i in senders):
                pairs.append((i, i + by))
        return lax.ppermute(value, "group", pairs)
    stride = (2 * sizes[1], 2, 1)[axis]
    for i in range(sizes[0] * sizes[1] * 2):
        at = (i // stride) % extent
        if 0 <= at + by < extent and (senders is None or at in senders):
            pairs.append((i, i + by * stride))
    return lax.ppermute(value, "dp", pairs)


def swap_along(value, axis, sizes):
    stride = (2 * sizes[1], 2, 1)[axis]
    count = sizes[0] * sizes[1] * 2
    pairs = [(i, i + stride * (1 - 2 * ((i // stride) % 2))) for i in range(count)]
    return lax.ppermute(value, "dp", pairs)


def gather_axis(value, axis, sizes):
    extent = sizes[axis]
    if extent == 2:
        return jnp.stack([value, swap_along(value, axis, sizes)])
    stride = (2 * sizes[1], 2, 1)[axis]
    count = sizes[0] * sizes[1] * 2
    groups = [
        [i + k * stride for k in range(extent)] for i in range(count) if (i // stride) % extent == 0
    ]
    return lax.all_gather(value, "dp", axis=0, axis_index_groups=groups)


def gather_pieces(line, sizes):
    head = line.shape[1] // 32 * 16
    pieces = []
    for part, order in ((line[:, :head], (1, 0)), (line[:, head:], (0, 1))):
        for axis in order:
            part = gather_axis(part, axis, sizes)
        part = part.reshape(-1, *part.shape[-2:])
        pieces += [part, swap_along(part, 2, sizes)]
    return pieces


def swap_line(value, bit, sizes):
    return lax.ppermute(value, "group", [(i, i ^ bit) for i in range(sizes[3])])


def pick(blocks, index, axis=0):
    return lax.dynamic_index_in_dim(blocks, index, axis=axis, keepdims=False)


def scatter_axis(blocks, axis, sizes, where):
    extent, at = (sizes[axis], where[axis])
    if extent == 1:
        return blocks[0].astype(jnp.float32)
    if extent == 2 and axis < 3:
        arrived = swap_along(pick(blocks, 1 - at), axis, sizes)
        return pick(blocks, at).astype(jnp.float32) + arrived.astype(jnp.float32)
    total = pick(blocks, at).astype(jnp.float32)
    for by in (1, -1):
        arrived = None
        for step in range(1, extent):
            dest = jnp.clip(at + by * (extent - step), 0, extent - 1)
            load = pick(blocks, dest)
            if arrived is not None:
                load = (load.astype(jnp.float32) + arrived.astype(jnp.float32)).astype(jnp.bfloat16)
            senders = range(step) if by == 1 else range(extent - step, extent)
            arrived = step_along(load, axis, by, sizes, senders)
        total = total + arrived.astype(jnp.float32)
    return total


def picked_sum(parts, index):
    if len(parts) == 1:
        return pick(parts[0], index)
    return sum(pick(part, index).astype(F32) for part in parts).astype(BF)


class Summing:
    def __init__(self, pair, sizes, where):
        self.send, self.keep = pair[:2], pair[2:]
        self.sizes, self.where, self.stage = sizes, where, 0

    def axes(self):
        return (0, 1) if self.stage == 1 else (1, 0)

    def loads(self):
        if self.stage == 0:
            return tuple(self.send)
        if self.stage <= 2:
            if self.sizes[0] != 2 or self.sizes[1] != 2:
                return ()
            near, far = self.axes()
            return (
                picked_sum(self.first, 1 - self.where[near]),
                picked_sum(self.second, 1 - self.where[far]),
            )
        return (self.side(1),)

    def side(self, other):
        index = lax.rem(self.where[3] // 2 ** (self.stage - 3) + other, 2)
        return pick(self.both.reshape(-1, 2, *self.both.shape[1:]), index, axis=1)

    def move(self, loads):
        if self.stage == 0:
            axes = (2, 2)
        elif self.stage <= 2:
            axes = self.axes()
        else:
            axes = (3,)
        result = []
        for load, axis in zip(loads, axes):
            if axis == 3:
                result.append(swap_line(load, 2 ** (self.stage - 3), self.sizes))
            else:
                result.append(swap_along(load, axis, self.sizes))
        return tuple(result)

    def add(self, arrived):
        if self.stage == 0:
            grid = (self.sizes[0], self.sizes[1], self.sizes[3])
            self.first, self.second = (
                tuple(part.reshape(grid + part.shape[1:]) for part in parts)
                for parts in zip(self.keep, arrived)
            )
            self.second = tuple(part.transpose(1, 0, 2, 3, 4) for part in self.second)
        elif self.stage <= 2:
            parts = []
            for i, (part, axis) in enumerate(zip((self.first, self.second), self.axes())):
                if arrived:
                    part = picked_sum(part, self.where[axis]).astype(F32) + arrived[i].astype(F32)
                else:
                    part = sum(one.astype(F32) for one in part).astype(BF)
                    part = scatter_axis(part, axis, self.sizes, self.where)
                parts.append(part.astype(BF))
            self.first, self.second = ((part,) for part in parts)
            if self.stage == 2:
                self.both = jnp.concatenate(parts, axis=1)
        else:
            total = self.side(0).astype(F32) + arrived[0].astype(F32)
            self.both = total.astype(BF)
            self.total = total
        self.stage += 1

    def result(self):
        return (self.total if self.sizes[3] > 1 else self.both.astype(F32))[0]


def after(value, other):
    return lax.optimization_barrier((value, other))[0]


def advance(*sums):
    loads = lax.optimization_barrier(tuple(one.loads() for one in sums))
    moved = tuple(one.move(load) for one, load in zip(sums, loads))
    for one, came in zip(sums, lax.optimization_barrier(moved)):
        one.add(came)


def tied(first, second):
    return lax.optimization_barrier((first, second))


def halo_tokens(tokens, reach):
    pieces = [tokens]
    for _ in range(reach):
        pieces.insert(0, passed_along(pieces[0], "group", 1))
    return jnp.concatenate(pieces, axis=0)


def halo_return(rows, own):
    reach = rows.shape[0] // own - 1
    carried = None
    for slot in range(reach):
        piece = rows[slot * own : (slot + 1) * own]
        if carried is not None:
            piece = (piece.astype(F32) + carried.astype(F32)).astype(BF)
        carried = passed_along(piece, "group", -1)
    return rows[reach * own :].astype(F32) + carried.astype(F32)


def shards(tokens, cotangent, positions, attn_weights, ffn_weights, attn_m, attn_v, ffn_m, ffn_v):
    sizes, where = grid_of()
    core = where[2].astype(jnp.int32).reshape(1)
    attn_own, ffn_own = (attn_weights.shape[0], ffn_weights.shape[0])
    devices = math.prod(sizes)
    own = tokens.shape[0]
    reach = (WINDOW - 1) // own + 1

    ffn_full = lax.all_gather(ffn_weights.astype(BF), ("dp", "group"), axis=0)
    window = halo_tokens(tokens, reach)
    place = positions[:, None]
    before = positions[0] + jnp.arange(-reach * own, 0, dtype=positions.dtype)
    cosine, sine_t = rope_tables(jnp.concatenate([before, positions]))

    block = jnp.pad(attn_weights.astype(BF), ((0, rows_up(attn_own) - attn_own), (0, 0)))
    line = lax.all_gather(block, "group", axis=0)
    here = jnp.stack(where).astype(jnp.int32)
    dims = attn_shapes()[:4]
    parts = unpack(
        functools.partial(unpack_pieces_body, dims, attn_own, sizes),
        dims,
        14,
        attn_own,
        devices,
        gather_pieces(line, sizes),
        (here,),
    )
    attn_parts = parts[:4] + cut_gains(parts[4], (D, HD, HD, D))
    normed_b, queries, keys, query_b, key_b, value_b, attended_b, branch, middle = attention(
        window, place, cosine, sine_t, attn_parts
    )

    ffn_full, middle = tied(ffn_full, middle)
    output, grad_middle, *pair = feed_forward(core, middle, cotangent, ffn_full, sizes)
    ffn_sum = Summing(pair, sizes, where)
    advance(ffn_sum)
    loads, grad_middle = tied(ffn_sum.loads(), grad_middle)
    moved = ffn_sum.move(loads)
    kept = (queries, keys, query_b, key_b, value_b)
    (
        grad_branch_b, grad_q_b, grad_k_b, grad_v_b, grad_normed, sum_in, sum_q, sum_k, sum_mid,
    ) = attention_back(grad_middle, branch, window, place, cosine, sine_t, kept, attn_parts)
    pair = pack_grads(
        attn_shapes()[:4],
        [normed_b, normed_b, normed_b, attended_b],
        [grad_q_b, grad_k_b, grad_v_b, grad_branch_b],
        [sum_in, sum_q, sum_k, sum_mid],
        attn_own,
        sizes,
        core,
    )
    ffn_sum.add(after(moved, pair))
    attn_sum = Summing(pair, sizes, where)
    last = 3 + (sizes[3] - 1).bit_length()
    while attn_sum.stage < last:
        moved = ffn_sum.move(ffn_sum.loads()) if ffn_sum.stage < last else None
        if attn_sum.stage == 0:
            attn_sum.add(attn_sum.move(attn_sum.loads()))
        loads = attn_sum.loads()
        if moved is not None:
            ffn_sum.add(after(moved, loads))
        attn_sum.add(attn_sum.move(loads))
    while ffn_sum.stage < last:
        ffn_sum.add(ffn_sum.move(ffn_sum.loads()))
    ffn_grad = ffn_sum.result()[:ffn_own]
    attn_grad = attn_sum.result()[:attn_own]

    grad_kv = halo_return(
        jnp.concatenate([grad_k_b, grad_v_b], axis=1), own
    ).astype(BF)
    w_k, w_v, g_in = attn_parts[1], attn_parts[2], attn_parts[4]
    grad_normed = (
        grad_normed + times_trans(grad_kv[:, :HD], w_k) + times_trans(grad_kv[:, HD:], w_v)
    )
    values = tokens.astype(F32)
    grad_tokens = grad_middle + norm_grad(values, row_norm(values), g_in, grad_normed)[0]
    attn_new, attn_m_new, attn_v_new = adam_step(attn_weights, attn_grad, attn_m, attn_v)
    ffn_new, ffn_m_new, ffn_v_new = adam_step(ffn_weights, ffn_grad, ffn_m, ffn_v)
    return (
        output,
        grad_tokens,
        attn_grad,
        ffn_grad,
        attn_new,
        ffn_new,
        attn_m_new,
        attn_v_new,
        ffn_m_new,
        ffn_v_new,
    )


def solution(mesh):
    placed = (
        P(("dp", "group"), None),
        P(("dp", "group"), None),
        P(("dp", "group")),
        P(("dp", "group"), None),
        P(("dp", "group"), None),
        P(("dp", "group"), None),
        P(("dp", "group"), None),
        P(("dp", "group"), None),
        P(("dp", "group"), None),
    )

    return jax.shard_map(
        shards,
        mesh=mesh,
        in_specs=placed,
        out_specs=(
            P(("dp", "group"), None),
            P(("dp", "group"), None),
            P(("dp", "group"), None),
            P(("dp", "group"), None),
            P(("dp", "group"), None),
            P(("dp", "group"), None),
            P(("dp", "group"), None),
            P(("dp", "group"), None),
            P(("dp", "group"), None),
            P(("dp", "group"), None),
        ),
        check_vma=False,
    )
```

```python
import functools
import math

import jax
import jax.numpy as jnp
from jax import lax
from jax.experimental import pallas as pl
from jax.experimental.pallas import tpu as pltpu
from jax.sharding import PartitionSpec as P


D = 640
H = 4
HD = 256
FF = 2048
WINDOW = 512
STEP = 3


NORM_EPS = 1e-06
THETA = 10000.0
BETA_ONE = 0.9
BETA_TWO = 0.95
LEARN_RATE = 0.02
WEIGHT_DECAY = 0.1
ADAM_EPS = 1e-08
GELU_COEF = 0.7978845608028654


def passed_along(shard, axis, by):
    count = lax.axis_size(axis)
    pairs = [(i, i + by) for i in range(count) if 0 <= i + by < count]
    return lax.ppermute(shard, axis, pairs)


def attn_shapes():
    return [(D, H * HD), (D, HD), (D, HD), (H * HD, D), (D,), (HD,), (HD,), (D,)]


def ffn_shapes():
    return [(D, FF), (D, FF), (FF, D), (D,), (D,)]


def rope_tables(positions):
    half_dim = HD // 2
    freqs = jnp.power(THETA, -2.0 * jnp.arange(half_dim, dtype=jnp.float32) / HD)
    angles = positions.astype(jnp.float32)[:, None] * freqs[None, :]
    return (jnp.cos(angles), jnp.sin(angles))


def gelu_pair(values):
    tangent = jnp.tanh(GELU_COEF * (values + 0.044715 * (values * values * values)))
    activated = 0.5 * values * (1.0 + tangent)
    slope_v = 0.5 * (1.0 + tangent) + 0.5 * values * (1.0 - tangent * tangent) * GELU_COEF * (
        1.0 + 3.0 * 0.044715 * values * values
    )
    return (activated, slope_v)


def times_trans(left, right):
    return lax.dot_general(
        left, right, (((1,), (1,)), ((), ())), preferred_element_type=jnp.float32
    )


def adam_step(param, grad_in, moment_one, moment_two):
    new_one = BETA_ONE * moment_one + (1.0 - BETA_ONE) * grad_in
    new_two = BETA_TWO * moment_two + (1.0 - BETA_TWO) * grad_in * grad_in
    corr_one = new_one / (1.0 - BETA_ONE**STEP)
    corr_two = new_two / (1.0 - BETA_TWO**STEP)
    new_param = param - LEARN_RATE * (
        corr_one / (jnp.sqrt(corr_two) + ADAM_EPS) + WEIGHT_DECAY * param
    )
    return (new_param, new_one, new_two)


BF = jnp.bfloat16
F32 = jnp.float32
VMEM_LIMIT = 60 * 1024 * 1024


def rows_up(count, unit=16):
    return -(-count // unit) * unit


def lay_out(jobs, lefts, rights, gains, flat):
    offset = 0
    tile = 128
    for (m, n), left, right in zip(jobs, lefts, rights):
        per_row = n // 128
        skip = left.shape[0] - right.shape[0]

        def step(i, carry, left=left, right=right, per_row=per_row, offset=offset, skip=skip):
            start = pl.multiple_of(i * tile, tile)
            block = contract(left[skip:, pl.ds(start, tile)], right[...], 0, 0)
            base = offset + i * (tile * per_row)
            for j in range(per_row):
                flat[pl.ds(base + j, tile, stride=per_row), :] = block[:, 128 * j : 128 * j + 128]
            return carry

        lax.fori_loop(0, m // tile, step, 0)
        offset = offset + m * per_row
    tail = flat.shape[0] - offset
    flat[pl.ds(offset, tail), :] = jnp.zeros((tail, 128), F32)
    for row in gains:
        for j in range(row.shape[1] // 128):
            flat[pl.ds(offset, 1), :] = row[:, 128 * j : 128 * j + 128]
            offset = offset + 1


def halves(padded):
    cut = padded // 32 * 16
    return (cut, padded - cut)


def cut_owners(flat, own, padded, sizes, core, outs):
    slow, fast, _, depth = sizes
    cut = halves(padded)[0]

    def step(i, carry):
        lead, z = i // depth, i % depth
        for which, (head, rest) in ((1 - core, outs[:2]), (core, outs[2:])):
            start = ((lead * 2 + which) * depth + z) * own
            block = flat[pl.ds(start, padded), :].astype(BF)
            head[i] = block[:cut]
            rest[i] = block[cut:]
        return carry

    lax.fori_loop(0, slow * fast * depth, step, 0)


def pack_body(jobs, own, padded, sizes, core_ref, *refs):
    count = len(jobs)
    lefts, rights, gains = refs[:count], refs[count : 2 * count], refs[2 * count : -5]
    outs, flat = refs[-5:-1], refs[-1]
    lay_out(jobs, lefts, rights, gains, flat)
    cut_owners(flat, own, padded, sizes, core_ref[0], outs)


def pack_grads(jobs, lefts, rights, gains, own, sizes, core):
    padded = rows_up(own)
    devices = math.prod(sizes)
    half = devices // 2
    whole = rows_up(devices * own + 16, 8)
    out = tuple(jax.ShapeDtypeStruct((half, rows, 128), BF) for rows in halves(padded)) * 2
    vmem = pl.BlockSpec(memory_space=pltpu.VMEM)
    flops = sum(2 * m * n * lefts[0].shape[0] for m, n in jobs)
    return pl.pallas_call(
        functools.partial(pack_body, jobs, own, padded, sizes),
        out_shape=out,
        in_specs=[pl.BlockSpec(memory_space=pltpu.SMEM)] + [vmem] * (2 * len(jobs) + len(gains)),
        out_specs=(vmem,) * 4,
        scratch_shapes=[pltpu.VMEM((whole, 128), F32)],
        compiler_params=pltpu.CompilerParams(vmem_limit_bytes=VMEM_LIMIT),
        cost_estimate=pl.CostEstimate(
            flops=flops, bytes_accessed=devices * padded * 256, transcendentals=0
        ),
    )(core, *lefts, *rights, *gains)


def spread(flat, dims_list, outs):
    offset = 0
    tile = 128
    for (m, n), out in zip(dims_list, outs):
        per_row = n // 128

        def step(i, carry, out=out, per_row=per_row, offset=offset):
            start = pl.multiple_of(i * tile, tile)
            base = offset + i * (tile * per_row)
            for j in range(per_row):
                piece = flat[pl.ds(base + j, tile, stride=per_row), :]
                out[pl.ds(start, tile), 128 * j : 128 * j + 128] = piece.astype(BF)
            return carry

        lax.fori_loop(0, m // tile, step, 0)
        offset = offset + m * per_row
    if len(outs) > len(dims_list):
        outs[-1][...] = flat[pl.ds(offset, outs[-1].shape[0]), :]
    return offset


def unpack_pieces_body(dims_list, own, sizes, at_ref, *refs):
    first, first_far, second, second_far = refs[:4]
    outs, flat = refs[4:-1], refs[-1]
    slow, fast, _, depth = sizes
    head = first.shape[1]
    near = tuple(at_ref[i] for i in range(3))

    def seen(extent, owner, here):
        return owner ^ here if extent == 2 else owner

    def put(i, carry):
        z, b, a = i % depth, (i // depth) % fast, i // (depth * fast)
        ra, rb = seen(slow, a, near[0]), seen(fast, b, near[1])
        one = (ra * fast + rb) * depth + z
        two = (rb * slow + ra) * depth + z
        for core, left, right in ((near[2], first, second), (1 - near[2], first_far, second_far)):
            base = (((a * fast + b) * 2 + core) * depth + z) * own
            flat[pl.ds(base, head), :] = left[one].astype(F32)
            flat[pl.ds(base + head, own - head), :] = right[two, : own - head].astype(F32)
        return carry

    lax.fori_loop(0, slow * fast * depth, put, 0)
    spread(flat, dims_list, outs)


def unpack(body, dims_list, gain_rows, own, devices, ins, scalars=()):
    vmem = pl.BlockSpec(memory_space=pltpu.VMEM)
    outs = [jax.ShapeDtypeStruct(dims, BF) for dims in dims_list]
    outs.append(jax.ShapeDtypeStruct((rows_up(gain_rows, 8), 128), F32))
    return pl.pallas_call(
        body,
        out_shape=tuple(outs),
        in_specs=[pl.BlockSpec(memory_space=pltpu.SMEM)] * len(scalars) + [vmem] * len(ins),
        out_specs=tuple([vmem] * len(outs)),
        scratch_shapes=[pltpu.VMEM((rows_up(devices * own + 8, 8), 128), F32)],
        compiler_params=pltpu.CompilerParams(vmem_limit_bytes=VMEM_LIMIT),
        cost_estimate=pl.CostEstimate(
            flops=0, bytes_accessed=devices * own * 512, transcendentals=0
        ),
    )(*scalars, *ins)


def contract(left, right, left_dim, right_dim):
    return lax.dot_general(
        left, right, (((left_dim,), (right_dim,)), ((), ())), preferred_element_type=F32
    )


def row_norm(values):
    return lax.rsqrt(jnp.mean(values * values, axis=-1, keepdims=True) + NORM_EPS)


def turn(values, cosine, sine_t, sign):
    first, second = values[:, : HD // 2], values[:, HD // 2 :]
    return jnp.concatenate(
        [first * cosine - sign * (second * sine_t), second * cosine + sign * (first * sine_t)],
        axis=-1,
    )


def seen_keys(reach, place, own, window):
    gap = lax.broadcasted_iota(jnp.int32, (own, window), 0) + (window - own)
    gap = gap - lax.broadcasted_iota(jnp.int32, (own, window), 1)
    return (gap >= 0) & (gap <= jnp.minimum(place, reach - 1))


def norm_grad(values, recip, gain, grad_out):
    scaled = grad_out * (1.0 + gain)
    grad_in = recip * scaled - values * recip * recip * recip * jnp.mean(
        scaled * values, axis=-1, keepdims=True
    )
    return grad_in, jnp.sum(grad_out * values * recip, axis=0, keepdims=True)


def attention_body(
    tokens, place, cosine, sine_t, w_q, w_k, w_v, w_o, g_in, g_q, g_k, g_mid,
    normed_b, queries, keys, query_b, key_b, value_b, attended_b, branch, middle,
):
    window, own = tokens.shape[0], place.shape[0]
    start = window - own
    values = tokens[...].astype(F32)
    normed_b[...] = (values * row_norm(values) * (1.0 + g_in[...])).astype(BF)
    keys[...] = contract(normed_b[...], w_k[...], 1, 0)
    value_b[...] = contract(normed_b[...], w_v[...], 1, 0).astype(BF)
    keyed = keys[...]
    keyed = keyed * row_norm(keyed) * (1.0 + g_k[...])
    key_b[...] = turn(keyed, cosine[...], sine_t[...], 1.0).astype(BF)
    queries[...] = contract(normed_b[start:, :], w_q[...], 1, 0)

    def head(h, carry):
        at = pl.ds(pl.multiple_of(h * HD, HD), HD)
        asked = queries[:, at]
        asked = asked * row_norm(asked) * (1.0 + g_q[...])
        asked = turn(asked, cosine[start:, :], sine_t[start:, :], 1.0) * (HD ** (-0.5))
        query_b[:, at] = asked.astype(BF)
        visible = seen_keys(WINDOW, place[...], own, window)
        scores = contract(query_b[:, at], key_b[...], 1, 1)
        total = jnp.sum(jnp.where(visible, jnp.exp(scores), 0.0), axis=-1, keepdims=True)
        prob = jnp.where(visible, jnp.exp(scores - jnp.log(total)), 0.0)
        attended_b[:, at] = contract(prob.astype(BF), value_b[...], 1, 0).astype(BF)
        return carry

    lax.fori_loop(0, H, head, 0)
    branch[...] = contract(attended_b[...], w_o[...], 1, 0)
    out = branch[...]
    middle[...] = values[start:, :] + out * row_norm(out) * (1.0 + g_mid[...])


def attention_back_body(
    grad_middle, branch, tokens, place, cosine, sine_t, queries, keys, query_b, key_b, value_b,
    w_q, w_k, w_v, w_o, g_in, g_q, g_k, g_mid,
    grad_branch_b, grad_q_b, grad_k_b, grad_v_b, grad_normed, sum_in, sum_q, sum_k, sum_mid,
    grad_key, grad_value,
):
    window, own = tokens.shape[0], place.shape[0]
    start = window - own
    out = branch[...]
    grad_branch, sum_mid[...] = norm_grad(out, row_norm(out), g_mid[...], grad_middle[...])
    grad_branch_b[...] = grad_branch.astype(BF)
    grad_key[...] = jnp.zeros_like(grad_key)
    grad_value[...] = jnp.zeros_like(grad_value)
    sum_q[...] = jnp.zeros_like(sum_q)

    def head(h, carry):
        at = pl.ds(pl.multiple_of(h * HD, HD), HD)
        grad_att = contract(grad_branch_b[...], w_o[at, :], 1, 1).astype(BF)
        visible = seen_keys(WINDOW, place[...], own, window)
        scores = contract(query_b[:, at], key_b[...], 1, 1)
        total = jnp.sum(jnp.where(visible, jnp.exp(scores), 0.0), axis=-1, keepdims=True)
        prob = jnp.where(visible, jnp.exp(scores - jnp.log(total)), 0.0)
        grad_prob = contract(grad_att, value_b[...], 1, 1)
        row_dot = jnp.sum(prob * grad_prob, axis=-1, keepdims=True)
        grad_score = (prob * (grad_prob - row_dot)).astype(BF)
        grad_query = contract(grad_score, key_b[...], 1, 0)
        grad_key[...] += contract(grad_score, query_b[:, at], 0, 0)
        grad_value[...] += contract(prob.astype(BF), grad_att, 0, 0)
        back = turn(grad_query * (HD ** (-0.5)), cosine[start:, :], sine_t[start:, :], -1.0)
        asked = queries[:, at]
        grad_q, part = norm_grad(asked, row_norm(asked), g_q[...], back)
        grad_q_b[:, at] = grad_q.astype(BF)
        sum_q[...] += part
        return carry

    lax.fori_loop(0, H, head, 0)
    keyed = keys[...]
    back = turn(grad_key[...], cosine[...], sine_t[...], -1.0)
    grad_k, sum_k[...] = norm_grad(keyed, row_norm(keyed), g_k[...], back)
    grad_k_b[...] = grad_k.astype(BF)
    grad_v_b[...] = grad_value[...].astype(BF)
    grad_normed[...] = contract(grad_q_b[...], w_q[...], 1, 1)
    through = contract(grad_k_b[...], w_k[...], 1, 1) + contract(grad_v_b[...], w_v[...], 1, 1)
    values = tokens[...].astype(F32)
    scaled = values * row_norm(values)
    sum_in[...] = jnp.sum(through * scaled, axis=0, keepdims=True) + jnp.sum(
        grad_normed[...] * scaled[start:, :], axis=0, keepdims=True
    )


def in_vmem(body, outs, scratch, flops, args):
    vmem = pl.BlockSpec(memory_space=pltpu.VMEM)
    out_shape = tuple(jax.ShapeDtypeStruct(shape, kind) for shape, kind in outs)
    moved = sum(math.prod(o.shape) * o.dtype.itemsize for o in (*out_shape, *args))
    return pl.pallas_call(
        body,
        out_shape=out_shape,
        in_specs=[vmem] * len(args),
        out_specs=tuple([vmem] * len(outs)),
        scratch_shapes=[pltpu.VMEM(shape, F32) for shape in scratch],
        compiler_params=pltpu.CompilerParams(vmem_limit_bytes=VMEM_LIMIT),
        cost_estimate=pl.CostEstimate(flops=flops, bytes_accessed=moved, transcendentals=0),
    )(*args)


def attention(tokens, place, cosine, sine_t, weights):
    window, own = tokens.shape[0], place.shape[0]
    outs = [
        ((window, D), BF), ((own, H * HD), F32), ((window, HD), F32), ((own, H * HD), BF),
        ((window, HD), BF), ((window, HD), BF), ((own, H * HD), BF), ((own, D), F32), ((own, D), F32),
    ]
    flops = 4 * own * window * H * HD + 4 * own * D * H * HD + 4 * window * D * HD
    return in_vmem(attention_body, outs, (), flops, (tokens, place, cosine, sine_t, *weights))


def attention_back(grad_middle, branch, tokens, place, cosine, sine_t, kept, weights):
    window, own = tokens.shape[0], place.shape[0]
    outs = [
        ((own, D), BF), ((own, H * HD), BF), ((window, HD), BF), ((window, HD), BF), ((own, D), F32),
        ((1, D), F32), ((1, HD), F32), ((1, HD), F32), ((1, D), F32),
    ]
    flops = 10 * own * window * H * HD + 4 * own * D * H * HD + 4 * window * D * HD
    args = (grad_middle, branch, tokens, place, cosine, sine_t, *kept, *weights)
    return in_vmem(attention_back_body, outs, ((window, HD), (window, HD)), flops, args)


def feed_forward_body(
    dims_list, own_rows, padded, sizes,
    core_ref, middle, top_in, blocks,
    output, grad_middle, send_head, send_rest, keep_head, keep_rest,
    flat, w_g, w_u, w_d, pre_b, hidden_b, grad_ffn_b, grad_gate_b, grad_upper_b, gate, upper, total,
):
    def put(d, carry):
        flat[pl.ds(d * own_rows, own_rows), :] = blocks[d].astype(F32)
        return carry

    lax.fori_loop(0, blocks.shape[0], put, 0)
    offset = spread(flat, dims_list, (w_g, w_u, w_d))
    rows = D // 128
    g_pre, g_post = (
        jnp.concatenate([flat[pl.ds(at + j, 1), :] for j in range(rows)], axis=1)
        for at in (offset, offset + rows)
    )
    tile = 512
    steps = gate.shape[1] // tile
    values = middle[...]
    recip = row_norm(values)
    pre_b[...] = (values * recip * (1.0 + g_pre)).astype(BF)
    total[...] = jnp.zeros_like(total)

    def forward(t, carry):
        at = pl.ds(pl.multiple_of(t * tile, tile), tile)
        gate_t = contract(pre_b[...], w_g[:, at], 1, 0)
        upper_t = contract(pre_b[...], w_u[:, at], 1, 0)
        gate[:, at] = gate_t
        upper[:, at] = upper_t
        activated, _ = gelu_pair(gate_t)
        hidden_b[:, at] = (activated * upper_t).astype(BF)
        total[...] += contract(hidden_b[:, at], w_d[at, :], 1, 0)
        return carry

    lax.fori_loop(0, steps, forward, 0)
    ffn_out = total[...]
    recip_post = row_norm(ffn_out)
    output[...] = (values + ffn_out * recip_post * (1.0 + g_post)).astype(BF)
    top = top_in[...].astype(F32)
    grad_ffn, sum_post = norm_grad(ffn_out, recip_post, g_post, top)
    grad_ffn_b[...] = grad_ffn.astype(BF)
    total[...] = jnp.zeros_like(total)

    def backward(t, carry):
        at = pl.ds(pl.multiple_of(t * tile, tile), tile)
        grad_hidden = contract(grad_ffn_b[...], w_d[at, :], 1, 1)
        activated, slope = gelu_pair(gate[:, at])
        grad_gate_b[:, at] = (grad_hidden * upper[:, at] * slope).astype(BF)
        grad_upper_b[:, at] = (grad_hidden * activated).astype(BF)
        total[...] += contract(grad_gate_b[:, at], w_g[:, at], 1, 1)
        total[...] += contract(grad_upper_b[:, at], w_u[:, at], 1, 1)
        return carry

    lax.fori_loop(0, steps, backward, 0)
    grad_add, sum_pre = norm_grad(values, recip, g_pre, total[...])
    grad_middle[...] = top + grad_add
    lay_out(
        dims_list,
        (pre_b, pre_b, hidden_b),
        (grad_gate_b, grad_upper_b, grad_ffn_b),
        (sum_pre, sum_post),
        flat,
    )
    outs = (send_head, send_rest, keep_head, keep_rest)
    cut_owners(flat, own_rows, padded, sizes, core_ref[0], outs)


def feed_forward(core, middle, cotangent, blocks, sizes):
    own = middle.shape[0]
    devices, own_rows = blocks.shape[:2]
    padded = rows_up(own_rows)
    dims_list = ffn_shapes()[:3]
    out = tuple(jax.ShapeDtypeStruct((devices // 2, rows, 128), BF) for rows in halves(padded)) * 2
    vmem = pl.BlockSpec(memory_space=pltpu.VMEM)
    scratch = [((rows_up(devices * own_rows + 16, 8), 128), F32)]
    scratch += [(dims, BF) for dims in dims_list]
    scratch += [((own, D), BF), ((own, FF), BF), ((own, D), BF), ((own, FF), BF), ((own, FF), BF)]
    scratch += [((own, FF), F32), ((own, FF), F32), ((own, D), F32)]
    return pl.pallas_call(
        functools.partial(feed_forward_body, dims_list, own_rows, padded, sizes),
        out_shape=(
            jax.ShapeDtypeStruct((own, D), BF), jax.ShapeDtypeStruct((own, D), F32), *out,
        ),
        in_specs=[pl.BlockSpec(memory_space=pltpu.SMEM)] + [vmem] * 3,
        out_specs=(vmem,) * 6,
        scratch_shapes=[pltpu.VMEM(shape, kind) for shape, kind in scratch],
        compiler_params=pltpu.CompilerParams(vmem_limit_bytes=VMEM_LIMIT),
        cost_estimate=pl.CostEstimate(
            flops=18 * own * D * FF, bytes_accessed=4 * blocks.size, transcendentals=own * FF
        ),
    )(core, middle, cotangent, blocks)


def cut_gains(rows, lengths):
    line = rows.reshape(-1)
    starts = [sum(lengths[:i]) for i in range(len(lengths))]
    return tuple(line[a : a + b].reshape(1, b) for a, b in zip(starts, lengths))


def grid_of():
    pairs = lax.axis_size("dp") // 2
    slow = math.isqrt(pairs)
    fast = pairs // slow
    depth = lax.axis_size("group")
    place = lax.axis_index("dp")
    where = (place // (2 * fast), (place // 2) % fast, place % 2, lax.axis_index("group"))
    return ((slow, fast, 2, depth), where)


def step_along(value, axis, by, sizes, senders=None):
    extent = sizes[axis]
    pairs = []
    if axis == 3:
        for i in range(extent):
            if 0 <= i + by < extent and (senders is None or i in senders):
                pairs.append((i, i + by))
        return lax.ppermute(value, "group", pairs)
    stride = (2 * sizes[1], 2, 1)[axis]
    for i in range(sizes[0] * sizes[1] * 2):
        at = (i // stride) % extent
        if 0 <= at + by < extent and (senders is None or at in senders):
            pairs.append((i, i + by * stride))
    return lax.ppermute(value, "dp", pairs)


def swap_along(value, axis, sizes):
    stride = (2 * sizes[1], 2, 1)[axis]
    count = sizes[0] * sizes[1] * 2
    pairs = [(i, i + stride * (1 - 2 * ((i // stride) % 2))) for i in range(count)]
    return lax.ppermute(value, "dp", pairs)


def gather_axis(value, axis, sizes):
    extent = sizes[axis]
    if extent == 2:
        return jnp.stack([value, swap_along(value, axis, sizes)])
    stride = (2 * sizes[1], 2, 1)[axis]
    count = sizes[0] * sizes[1] * 2
    groups = [
        [i + k * stride for k in range(extent)] for i in range(count) if (i // stride) % extent == 0
    ]
    return lax.all_gather(value, "dp", axis=0, axis_index_groups=groups)


def gather_pieces(line, sizes):
    head = line.shape[1] // 32 * 16
    pieces = []
    for part, order in ((line[:, :head], (1, 0)), (line[:, head:], (0, 1))):
        for axis in order:
            part = gather_axis(part, axis, sizes)
        part = part.reshape(-1, *part.shape[-2:])
        pieces += [part, swap_along(part, 2, sizes)]
    return pieces


def swap_line(value, bit, sizes):
    return lax.ppermute(value, "group", [(i, i ^ bit) for i in range(sizes[3])])


def pick(blocks, index, axis=0):
    return lax.dynamic_index_in_dim(blocks, index, axis=axis, keepdims=False)


def scatter_axis(blocks, axis, sizes, where):
    extent, at = (sizes[axis], where[axis])
    if extent == 1:
        return blocks[0].astype(jnp.float32)
    if extent == 2 and axis < 3:
        arrived = swap_along(pick(blocks, 1 - at), axis, sizes)
        return pick(blocks, at).astype(jnp.float32) + arrived.astype(jnp.float32)
    total = pick(blocks, at).astype(jnp.float32)
    for by in (1, -1):
        arrived = None
        for step in range(1, extent):
            dest = jnp.clip(at + by * (extent - step), 0, extent - 1)
            load = pick(blocks, dest)
            if arrived is not None:
                load = (load.astype(jnp.float32) + arrived.astype(jnp.float32)).astype(jnp.bfloat16)
            senders = range(step) if by == 1 else range(extent - step, extent)
            arrived = step_along(load, axis, by, sizes, senders)
        total = total + arrived.astype(jnp.float32)
    return total


def picked_sum(parts, index):
    if len(parts) == 1:
        return pick(parts[0], index)
    return sum(pick(part, index).astype(F32) for part in parts).astype(BF)


class Summing:
    def __init__(self, pair, sizes, where):
        self.send, self.keep = pair[:2], pair[2:]
        self.sizes, self.where, self.stage = sizes, where, 0

    def axes(self):
        return (0, 1) if self.stage == 1 else (1, 0)

    def loads(self):
        return self.leaving()

    def leaving(self):
        if self.stage == 0:
            return tuple(self.send)
        if self.stage <= 2:
            if self.sizes[0] != 2 or self.sizes[1] != 2:
                return ()
            near, far = self.axes()
            return (
                picked_sum(self.first, 1 - self.where[near]),
                picked_sum(self.second, 1 - self.where[far]),
            )
        return (self.side(1),)

    def side(self, other):
        index = lax.rem(self.where[3] // 2 ** (self.stage - 3) + other, 2)
        return pick(self.both.reshape(-1, 2, *self.both.shape[1:]), index, axis=1)

    def move(self, loads):
        if self.stage == 0:
            axes = (2, 2)
        elif self.stage <= 2:
            axes = self.axes()
        else:
            axes = (3,)
        result = []
        for load, axis in zip(loads, axes):
            if axis == 3:
                result.append(swap_line(load, 2 ** (self.stage - 3), self.sizes))
            else:
                result.append(swap_along(load, axis, self.sizes))
        return tuple(result)

    def add(self, arrived):
        if self.stage == 0:
            grid = (self.sizes[0], self.sizes[1], self.sizes[3])
            self.first, self.second = (
                tuple(part.reshape(grid + part.shape[1:]) for part in parts)
                for parts in zip(self.keep, arrived)
            )
            self.second = tuple(part.transpose(1, 0, 2, 3, 4) for part in self.second)
        elif self.stage <= 2:
            parts = []
            for i, (part, axis) in enumerate(zip((self.first, self.second), self.axes())):
                if arrived:
                    part = picked_sum(part, self.where[axis]).astype(F32) + arrived[i].astype(F32)
                else:
                    part = sum(one.astype(F32) for one in part).astype(BF)
                    part = scatter_axis(part, axis, self.sizes, self.where)
                parts.append(part.astype(BF))
            self.first, self.second = ((part,) for part in parts)
            if self.stage == 2:
                self.both = jnp.concatenate(parts, axis=1)
        else:
            total = self.side(0).astype(F32) + arrived[0].astype(F32)
            self.both = total.astype(BF)
            self.total = total
        self.stage += 1

    def result(self):
        return (self.total if self.sizes[3] > 1 else self.both.astype(F32))[0]


def after(value, other):
    return lax.optimization_barrier((value, other))[0]


def tied(first, second):
    return lax.optimization_barrier((first, second))


def halo_tokens(tokens, reach):
    pieces = [tokens]
    for _ in range(reach):
        pieces.insert(0, passed_along(pieces[0], "group", 1))
    return jnp.concatenate(pieces, axis=0)


def halo_return(rows, own):
    reach = rows.shape[0] // own - 1
    carried = None
    for slot in range(reach):
        piece = rows[slot * own : (slot + 1) * own]
        if carried is not None:
            piece = (piece.astype(F32) + carried.astype(F32)).astype(BF)
        carried = passed_along(piece, "group", -1)
    return rows[reach * own :].astype(F32) + carried.astype(F32)


def shards(tokens, cotangent, positions, attn_weights, ffn_weights, attn_m, attn_v, ffn_m, ffn_v):
    sizes, where = grid_of()
    core = where[2].astype(jnp.int32).reshape(1)
    attn_own, ffn_own = (attn_weights.shape[0], ffn_weights.shape[0])
    devices = math.prod(sizes)
    own = tokens.shape[0]
    reach = (WINDOW - 1) // own + 1

    ffn_full = lax.all_gather(ffn_weights.astype(BF), ("dp", "group"), axis=0)
    window = halo_tokens(tokens, reach)
    place = positions[:, None]
    before = positions[0] + jnp.arange(-reach * own, 0, dtype=positions.dtype)
    cosine, sine_t = rope_tables(jnp.concatenate([before, positions]))

    block = jnp.pad(attn_weights.astype(BF), ((0, rows_up(attn_own) - attn_own), (0, 0)))
    line = lax.all_gather(block, "group", axis=0)
    here = jnp.stack(where).astype(jnp.int32)
    dims = attn_shapes()[:4]
    parts = unpack(
        functools.partial(unpack_pieces_body, dims, attn_own, sizes),
        dims,
        14,
        attn_own,
        devices,
        gather_pieces(line, sizes),
        (here,),
    )
    attn_parts = parts[:4] + cut_gains(parts[4], (D, HD, HD, D))
    normed_b, queries, keys, query_b, key_b, value_b, attended_b, branch, middle = attention(
        window, place, cosine, sine_t, attn_parts
    )

    ffn_full, middle = tied(ffn_full, middle)
    output, grad_middle, *pair = feed_forward(core, middle, cotangent, ffn_full, sizes)
    ffn_sum = Summing(pair, sizes, where)
    ffn_sum.add(ffn_sum.move(ffn_sum.loads()))
    moved = ffn_sum.move(ffn_sum.loads())
    kept = (queries, keys, query_b, key_b, value_b)
    (
        grad_branch_b, grad_q_b, grad_k_b, grad_v_b, grad_normed, sum_in, sum_q, sum_k, sum_mid,
    ) = attention_back(grad_middle, branch, window, place, cosine, sine_t, kept, attn_parts)
    pair = pack_grads(
        attn_shapes()[:4],
        [normed_b, normed_b, normed_b, attended_b],
        [grad_q_b, grad_k_b, grad_v_b, grad_branch_b],
        [sum_in, sum_q, sum_k, sum_mid],
        attn_own,
        sizes,
        core,
    )
    ffn_sum.add(after(moved, pair))
    attn_sum = Summing(pair, sizes, where)
    last = 3 + (sizes[3] - 1).bit_length()
    while attn_sum.stage < last:
        moved = ffn_sum.move(ffn_sum.loads()) if ffn_sum.stage < last else None
        if attn_sum.stage == 0:
            attn_sum.add(attn_sum.move(attn_sum.loads()))
        loads = attn_sum.loads()
        if moved is not None:
            ffn_sum.add(after(moved, loads))
        attn_sum.add(attn_sum.move(loads))
    while ffn_sum.stage < last:
        ffn_sum.add(ffn_sum.move(ffn_sum.loads()))
    ffn_grad = ffn_sum.result()[:ffn_own]
    attn_grad = attn_sum.result()[:attn_own]

    grad_kv = halo_return(
        jnp.concatenate([grad_k_b, grad_v_b], axis=1), own
    ).astype(BF)
    w_k, w_v, g_in = attn_parts[1], attn_parts[2], attn_parts[4]
    grad_normed = (
        grad_normed + times_trans(grad_kv[:, :HD], w_k) + times_trans(grad_kv[:, HD:], w_v)
    )
    values = tokens.astype(F32)
    grad_tokens = grad_middle + norm_grad(values, row_norm(values), g_in, grad_normed)[0]
    attn_new, attn_m_new, attn_v_new = adam_step(attn_weights, attn_grad, attn_m, attn_v)
    ffn_new, ffn_m_new, ffn_v_new = adam_step(ffn_weights, ffn_grad, ffn_m, ffn_v)
    return (
        output,
        grad_tokens,
        attn_grad,
        ffn_grad,
        attn_new,
        ffn_new,
        attn_m_new,
        attn_v_new,
        ffn_m_new,
        ffn_v_new,
    )


def solution(mesh):
    placed = (
        P(("dp", "group"), None),
        P(("dp", "group"), None),
        P(("dp", "group")),
        P(("dp", "group"), None),
        P(("dp", "group"), None),
        P(("dp", "group"), None),
        P(("dp", "group"), None),
        P(("dp", "group"), None),
        P(("dp", "group"), None),
    )

    return jax.shard_map(
        shards,
        mesh=mesh,
        in_specs=placed,
        out_specs=(
            P(("dp", "group"), None),
            P(("dp", "group"), None),
            P(("dp", "group"), None),
            P(("dp", "group"), None),
            P(("dp", "group"), None),
            P(("dp", "group"), None),
            P(("dp", "group"), None),
            P(("dp", "group"), None),
            P(("dp", "group"), None),
            P(("dp", "group"), None),
        ),
        check_vma=False,
    )
```
